512 devices in a mesh: tm: 32 (over x, y, core), col: 16 (over z).
Axes of the slice: x: 4, y: 4, z: 16, core: 2. Of those that a mesh axis runs over, the one named last changes fastest.
Arguments:
- initial: float32 [512], replicated, may hold values from 1 to 3
- offsets: int32 [512, 4], P('tm'), may hold values from -32 to 32
- upwind: int32 [512, 512], P('tm'), may hold values from 0 to 3
- courant: float32 [512, 512], P('tm'), may hold values from 0.02 to 0.4
- obs_cells: int32 [512, 64], P('tm'), may hold values from 0 to 511
- gains: float32 [512, 64, 512], P('tm'), may hold values from -0.05 to 0.05
- observed: float32 [512, 64], P('tm'), may hold values from -1 to 5
- smooth_gain: float32 [512, 512], P('tm'), may hold values from 0.3 to 1
Outputs:
- filtered: float32 [512, 512], P('tm')
- smoothed: float32 [512, 512], P('tm')
The draws below stay inside these ranges and needn't reach their ends.
All inputs are finite; a program needn't handle non-finite values.
Results may differ from the reference program's by a relative error of at most 0.0003.
Values sent between devices are 32-bit elements; how exact they have to be, the bound alone decides.
No kernel may reach another device: no remote copies, remote signals or barrier semaphores. Data moves between devices by JAX's collectives and lax.ppermute only.
A program may use at most 64 MiB of HBM per device.

```python
import math
import jax
import jax.numpy as jnp
from jax import lax

STATE_CELLS = 512
OBS = 64
BANDS = 4
MAXOFF = 32
HOURLY_STEPS = 512


def draw_smooth_gain(key, part):
    root_key, sudden_key, select_key = jax.random.split(jax.random.fold_in(key, 7), 3)
    constant_gain = jax.random.uniform(root_key, (HOURLY_STEPS, STATE_CELLS), jnp.float32, 0.996, 1.0)
    chance = 1.0 / 256.0
    sudden_gain = jax.random.uniform(sudden_key, (HOURLY_STEPS, STATE_CELLS), jnp.float32, 0.3, 0.9)
    selected = jax.random.uniform(select_key, (HOURLY_STEPS, STATE_CELLS), jnp.float32) < chance
    return jnp.where(selected, sudden_gain, constant_gain)


def touch_ends(entries, rng, low, largest):
    index_at = [jax.random.randint(jax.random.fold_in(rng, axis), (), 0, length) for axis, length in enumerate(entries.shape)]
    main_axis = entries.shape.index(max(entries.shape))
    next_to = index_at[:main_axis] + [(index_at[main_axis] + 1) % entries.shape[main_axis]] + index_at[main_axis + 1:]
    return entries.at[tuple(index_at)].set(low).at[tuple(next_to)].set(largest)


def block_scale(key, extent, cuts, low, high):
    def one(dim, blocks):
        heights = jax.random.uniform(jax.random.fold_in(jax.random.fold_in(key, 6), dim), (blocks,), jnp.float32, low / len(cuts), high / len(cuts))
        return jnp.repeat(jnp.exp(heights), extent[dim] // blocks).reshape((-1,) + (1,) * (len(extent) - dim - 1))

    factor_of = one(*cuts[0])
    for cut in cuts[1:]:
        factor_of = factor_of * one(*cut)
    return factor_of


def gaussian(rng, dims, deviation, most, cuts=(), kind=jnp.bfloat16):
    gain = block_scale(rng, dims, cuts, -0.22, 0.18) if cuts else 1.0
    values = jax.random.normal(rng, dims, jnp.float32) * deviation * gain
    return jnp.minimum(jnp.maximum(values, -most), most).astype(kind)


def setup_inputs(seed: int = 0) -> dict:
    key_list = jax.random.split(jax.random.key(seed), 9)
    return {
        "initial": jnp.clip(jax.random.uniform(key_list[0], (STATE_CELLS,), jnp.float32, 1.0, 3.0), 1.0, 3.0),
        "offsets": touch_ends(jax.random.randint(key_list[1], (HOURLY_STEPS, BANDS), 0 - MAXOFF, MAXOFF + 1), jax.random.fold_in(key_list[1], 1), 0 - MAXOFF, MAXOFF).astype(jnp.int32),
        "upwind": touch_ends(jax.random.randint(key_list[2], (HOURLY_STEPS, STATE_CELLS), 0, BANDS), jax.random.fold_in(key_list[2], 1), 0, BANDS - 1).astype(jnp.int32),
        "courant": jnp.clip(jnp.exp(math.log(0.4) - 2.9957323 * jax.random.uniform(key_list[3], (HOURLY_STEPS, STATE_CELLS), jnp.float32) ** block_scale(key_list[3], (HOURLY_STEPS, STATE_CELLS), ((0, 32),), -0.2, 0.2)), 0.02, 0.4),
        "obs_cells": touch_ends(jax.random.randint(key_list[4], (HOURLY_STEPS, OBS), 0, STATE_CELLS), jax.random.fold_in(key_list[4], 1), 0, STATE_CELLS - 1).astype(jnp.int32),
        "gains": gaussian(key_list[5], (HOURLY_STEPS, OBS, STATE_CELLS), 0.01, 0.05, ((0, 32),), jnp.float32),
        "observed": jnp.clip(-1.0 + 6.0 * jax.random.uniform(key_list[6], (HOURLY_STEPS, OBS), jnp.float32) ** block_scale(key_list[6], (HOURLY_STEPS, OBS), ((0, 32),), -0.2, 0.2), -1.0, 5.0),
        "smooth_gain": draw_smooth_gain(jax.random.fold_in(key_list[8], 71), 0),
    }


HIGHEST_PRECISION = lax.Precision.HIGHEST
DIFFUSION = 0.25
RELAXATION = 0.02


def shifted(values, offset):
    widths = [(0, 0)] * (values.ndim - 1) + [(MAXOFF, MAXOFF)]
    padded = jnp.pad(values, widths)
    return lax.dynamic_slice_in_dim(padded, MAXOFF + offset, STATE_CELLS, values.ndim - 1)


def transition(values, offsets, upwind, courant):
    result = (1.0 - courant - DIFFUSION) * values + 0.5 * DIFFUSION * (shifted(values, 1) + shifted(values, -1))
    for band in range(BANDS):
        weight = jnp.where(upwind == band, courant, 0.0)
        result = result + weight * shifted(values, offsets[band])
    return result


def transpose_apply(values, offsets, upwind, courant):
    result = (1.0 - courant - DIFFUSION) * values + 0.5 * DIFFUSION * (shifted(values, 1) + shifted(values, -1))
    for band in range(BANDS):
        weight = jnp.where(upwind == band, courant, 0.0)
        result = result + shifted(weight * values, 0 - offsets[band])
    return result


def observe(predicted, obs_cells, gains, observed):
    innovation = predicted[..., obs_cells] - observed
    corrected = predicted.at[..., obs_cells].add(-RELAXATION * innovation)
    return corrected - jnp.dot(innovation, gains, precision=HIGHEST_PRECISION)


def filter_step(current, offsets, upwind, courant, obs_cells, gains, observed):
    return observe(transition(current, offsets, upwind, courant), obs_cells, gains, observed)


def smooth_step(current, offsets, upwind, courant, smooth_gain, previous):
    mismatch = current - transition(previous, offsets, upwind, courant)
    return previous + smooth_gain * transpose_apply(mismatch, offsets, upwind, courant)


def reference(initial, offsets, upwind, courant, obs_cells, gains, observed, smooth_gain):
    def forward(current, inputs):
        current = filter_step(current, *inputs)
        return current, current

    final, filtered = lax.scan(forward, initial, (offsets, upwind, courant, obs_cells, gains, observed))
    previous = jnp.concatenate([initial[None, :], filtered[:-1]], axis=0)

    def backward(current, inputs):
        return smooth_step(current, *inputs), current

    _, smoothed = lax.scan(backward, final, (offsets, upwind, courant, smooth_gain, previous), reverse=True)
    return filtered, smoothed
```

```python
import functools

import jax
import jax.numpy as jnp
from jax import lax
from jax.experimental import pallas as pl
from jax.experimental.pallas import tpu as pltpu
from jax.sharding import PartitionSpec as P

N = 512
OBS = 64
BANDS = 4
DIFFUSION = 0.25
RELAXATION = 0.02
ROWS = N + 8
F32 = jnp.float32
BF16 = jnp.bfloat16
NT = (((1,), (1,)), ((), ()))
NN = (((1,), (0,)), ((), ()))


def lanes(rows):
    return lax.broadcasted_iota(jnp.int32, (rows, N), 1)


def back(off):
    return jnp.where(off > 0, N - off, -off)


def step_weights(offs, up, courant):
    reach = jnp.full_like(up, offs[0])
    for band in range(1, BANDS):
        reach = jnp.where(up == band, offs[band], reach)
    at = lanes(1) + reach
    inside = (at >= 0) & (at < N)
    return 1.0 - courant - DIFFUSION, jnp.where(inside, courant, 0.0)


def neighbours(v):
    lane = lanes(1)
    left = jnp.where(lane > 0, 0.5 * DIFFUSION, 0.0)
    right = jnp.where(lane < N - 1, 0.5 * DIFFUSION, 0.0)
    return right * pltpu.roll(v, N - 1, 1) + left * pltpu.roll(v, 1, 1)


def transition(v, offs, up, centre, adv):
    moved = pltpu.roll(v, back(offs[0]), 1)
    for band in range(1, BANDS):
        moved = jnp.where(up == band, pltpu.roll(v, back(offs[band]), 1), moved)
    return centre * v + neighbours(v) + adv * moved


def transpose_apply(v, offs, up, centre, adv):
    total = centre * v + neighbours(v)
    out = adv * v
    for band in range(BANDS):
        total = total + pltpu.roll(jnp.where(up == band, out, 0.0), back(-offs[band]), 1)
    return total


def split2(v):
    hi = v.astype(BF16)
    return hi, (v - hi.astype(F32)).astype(BF16)


def split3(v):
    hi = v.astype(BF16)
    rest = v - hi.astype(F32)
    mid = rest.astype(BF16)
    return hi, mid, (rest - mid.astype(F32)).astype(BF16)


def dot(a, b, dims=NN):
    return lax.dot_general(a, b, dims, preferred_element_type=F32)


def dot3(a, b):
    ah, al = split2(a)
    bh, bl = split2(b)
    return dot(ah, bh) + (dot(ah, bl) + dot(al, bh))


def observed_part(p, s4):
    hi, mid, lo = split3(p)
    return dot(hi, s4, NT) + (dot(mid, s4, NT) + dot(lo, s4, NT))


def gain_rows(s, gains):
    hi, lo = split2(RELAXATION * s.astype(F32) + gains)
    return jnp.concatenate([hi, hi, lo, lo], axis=0)


def correction(e4, kk):
    hi, lo = split2(e4)
    lane = lax.broadcasted_iota(jnp.int32, e4.shape, 1)
    odd = (lane // OBS) % 2 == 1
    return dot(jnp.where(odd, lo.astype(F32), hi.astype(F32)).astype(BF16), kk)


def one_hots(obs_t_ref, s_ref, steps):
    lane = lanes(OBS)
    for k in range(steps):
        s_ref[k] = jnp.where(obs_t_ref[:, k : k + 1] == lane, 1.0, 0.0).astype(BF16)


def read_step(k, offs_ref, up_ref, c_ref):
    offs = [offs_ref[k, band] for band in range(BANDS)]
    up = up_ref[pl.ds(k, 1), :]
    centre, adv = step_weights(offs, up, c_ref[pl.ds(k, 1), :])
    return offs, up, centre, adv


def vmem():
    return pl.BlockSpec(memory_space=pltpu.VMEM)


def smem():
    return pl.BlockSpec(memory_space=pltpu.SMEM)


def filter_map(offsets, upwind, courant, obs_t, gains, y4):
    steps, chunk = offsets.shape[0], 128

    def kernel(offs_ref, up_ref, c_ref, obs_t_ref, gains_ref, y4_ref, map_ref, s_ref):
        one_hots(obs_t_ref, s_ref, steps)
        row = lax.broadcasted_iota(jnp.int32, (ROWS, N), 0)
        map_ref[...] = jnp.where(row == lanes(ROWS), 1.0, 0.0)
        first = lax.broadcasted_iota(jnp.int32, (8, 1), 0) == 0

        def one(k, carry):
            offs, up, centre, adv = read_step(k, offs_ref, up_ref, c_ref)
            s = s_ref[k]
            kk = gain_rows(s, gains_ref[k])
            s4 = jnp.concatenate([s] * 4, axis=0)
            for r in range(0, N, chunk):
                at = pl.ds(r, chunk)
                p = transition(map_ref[at, :], offs, up, centre, adv)
                map_ref[at, :] = p - correction(observed_part(p, s4), kk)
            tail = pl.ds(N, 8)
            p = transition(map_ref[tail, :], offs, up, centre, adv)
            e4 = observed_part(p, s4) - jnp.where(first, y4_ref[pl.ds(k, 1), :], 0.0)
            map_ref[tail, :] = p - correction(e4, kk)
            return carry

        lax.fori_loop(0, steps, one, 0)

    return pl.pallas_call(
        kernel,
        out_shape=jax.ShapeDtypeStruct((ROWS, N), F32),
        in_specs=[smem()] + [vmem()] * 5,
        out_specs=vmem(),
        scratch_shapes=[pltpu.VMEM((steps, OBS, N), BF16)],
        cost_estimate=pl.CostEstimate(flops=16 * 10**9, bytes_accessed=4 << 20, transcendentals=0),
        name="filter_map",
    )(offsets, upwind, courant, obs_t, gains, y4)


def smoother_map(offsets, upwind, courant, smooth_gain):
    steps, chunk = offsets.shape[0], 64

    def kernel(offs_ref, up_ref, c_ref, sg_ref, map_ref):
        row = lax.broadcasted_iota(jnp.int32, (N, N), 0)
        map_ref[...] = jnp.where(row == lanes(N), 1.0, 0.0)

        def one(i, carry):
            k = steps - 1 - i
            offs, up, centre, adv = read_step(k, offs_ref, up_ref, c_ref)
            gain = sg_ref[pl.ds(k, 1), :]
            for r in range(0, N, chunk):
                at = pl.ds(r, chunk)
                map_ref[at, :] = gain * transpose_apply(map_ref[at, :], offs, up, centre, adv)
            return carry

        lax.fori_loop(0, steps, one, 0)

    return pl.pallas_call(
        kernel,
        out_shape=jax.ShapeDtypeStruct((N, N), F32),
        in_specs=[smem()] + [vmem()] * 3,
        out_specs=vmem(),
        cost_estimate=pl.CostEstimate(flops=8 * 10**9, bytes_accessed=1 << 20, transcendentals=0),
        name="smoother_map",
    )(offsets, upwind, courant, smooth_gain)


def forward(offsets, upwind, courant, obs_t, gains, y4, start):
    steps = offsets.shape[0]

    def kernel(offs_ref, up_ref, c_ref, obs_t_ref, gains_ref, y4_ref, start_ref, filt_ref, upd_ref, vec_ref, s_ref):
        one_hots(obs_t_ref, s_ref, steps)
        first = lax.broadcasted_iota(jnp.int32, (8, 1), 0) == 0
        vec_ref[...] = start_ref[...]

        def one(k, carry):
            offs, up, centre, adv = read_step(k, offs_ref, up_ref, c_ref)
            s = s_ref[k]
            kk = gain_rows(s, gains_ref[k])
            s4 = jnp.concatenate([s] * 4, axis=0)
            p = transition(vec_ref[...], offs, up, centre, adv)
            e4 = observed_part(p, s4) - jnp.where(first, y4_ref[pl.ds(k, 1), :], 0.0)
            update = -correction(e4, kk)
            vec_ref[...] = p + update
            filt_ref[pl.ds(k, 1), :] = (p + update)[0:1]
            upd_ref[pl.ds(k, 1), :] = update[0:1]
            return carry

        lax.fori_loop(0, steps, one, 0)

    out = jax.ShapeDtypeStruct((steps, N), F32)
    return pl.pallas_call(
        kernel,
        out_shape=(out, out),
        in_specs=[smem()] + [vmem()] * 6,
        out_specs=(vmem(), vmem()),
        scratch_shapes=[pltpu.VMEM((8, N), F32), pltpu.VMEM((steps, OBS, N), BF16)],
        cost_estimate=pl.CostEstimate(flops=4 * 10**9, bytes_accessed=2 << 20, transcendentals=0),
        name="forward",
    )(offsets, upwind, courant, obs_t, gains, y4, start)


def smooth(offsets, upwind, courant, smooth_gain, updates, filtered, top):
    steps = offsets.shape[0]

    def kernel(offs_ref, up_ref, c_ref, sg_ref, u_ref, x_ref, top_ref, out_ref, end_ref):
        def one(i, diff):
            k = steps - 1 - i
            offs, up, centre, adv = read_step(k, offs_ref, up_ref, c_ref)
            at = pl.ds(k, 1)
            out_ref[at, :] = x_ref[at, :] + diff[0:1]
            return sg_ref[at, :] * transpose_apply(diff + u_ref[at, :], offs, up, centre, adv)

        end_ref[...] = lax.fori_loop(0, steps, one, top_ref[...])

    return pl.pallas_call(
        kernel,
        out_shape=(jax.ShapeDtypeStruct((steps, N), F32), jax.ShapeDtypeStruct((8, N), F32)),
        in_specs=[smem()] + [vmem()] * 6,
        out_specs=(vmem(), vmem()),
        cost_estimate=pl.CostEstimate(flops=10**9, bytes_accessed=1 << 18, transcendentals=0),
        name="smooth",
    )(offsets, upwind, courant, smooth_gain, updates, filtered, top)


def compose(flag, mine, other):
    rows = mine.shape[0]

    def kernel(flag_ref, mine_ref, other_ref, out_ref):
        def product(a_ref, b_ref):
            bh, bl = split2(b_ref[0:N, :])
            for r in range(0, rows, 104 if rows == ROWS else 128):
                at = pl.ds(r, 104 if rows == ROWS else 128)
                ah, al = split2(a_ref[at, :])
                out_ref[at, :] = dot(ah, bh) + (dot(ah, bl) + dot(al, bh))
            if rows == ROWS:
                out_ref[N:ROWS, :] = out_ref[N:ROWS, :] + b_ref[N:ROWS, :]

        @pl.when(flag_ref[0] == 1)
        def _():
            product(other_ref, mine_ref)

        @pl.when(flag_ref[0] == 0)
        def _():
            product(mine_ref, other_ref)

    return pl.pallas_call(
        kernel,
        out_shape=jax.ShapeDtypeStruct((rows, N), F32),
        in_specs=[smem(), vmem(), vmem()],
        out_specs=vmem(),
        cost_estimate=pl.CostEstimate(flops=10**9, bytes_accessed=3 << 20, transcendentals=0),
        name="compose",
    )(flag, mine, other)


def through(state, maps, offset):
    def kernel(v_ref, m_ref, o_ref, out_ref):
        out_ref[...] = dot3(v_ref[...], m_ref[0:N, :]) + o_ref[...]

    return pl.pallas_call(
        kernel,
        out_shape=jax.ShapeDtypeStruct((8, N), F32),
        in_specs=[vmem()] * 3,
        out_specs=vmem(),
        cost_estimate=pl.CostEstimate(flops=10**8, bytes_accessed=1 << 20, transcendentals=0),
        name="through",
    )(state, maps, offset)


def on_device(initial, offsets, upwind, courant, obs_cells, gains, observed, smooth_gain):
    place = lax.axis_index("tm")
    x, y, core = place // 8, (place // 2) % 4, place % 2

    def moved(values, to, senders):
        return lax.ppermute(values, "tm", [(i, to(i)) for i in range(32) if senders(i)])

    even = lambda i: i % 2 == 0
    odd = lambda i: i % 2 == 1
    flag = lambda on: on.astype(jnp.int32).reshape(1)
    never = jnp.zeros((1,), jnp.int32)

    obs_t = obs_cells.T
    y4 = jnp.tile(observed, (1, 4))
    start_row = jnp.broadcast_to(initial[None, :], (8, N))
    zeros = jnp.zeros((8, N), F32)

    fmap = filter_map(offsets, upwind, courant, obs_t, gains, y4)
    fmap_odd = moved(fmap, lambda i: i - 1, odd)
    smap = smoother_map(offsets, upwind, courant, smooth_gain)
    fpair = compose(never, fmap, fmap_odd)
    fpair_other = moved(fpair, lambda i: i ^ 2, even)
    smap_even = moved(smap, lambda i: i + 1, even)
    spair = compose(never, smap, smap_even)
    fquad = compose(flag(y % 2 == 1), fpair, fpair_other)
    fquad_other = moved(fquad, lambda i: i ^ 4, even)
    spair_other = moved(spair, lambda i: i ^ 2, odd)
    foct = compose(flag(y >= 2), fquad, fquad_other)
    squad = compose(flag(y % 2 == 0), spair, spair_other)
    squad_other = moved(squad, lambda i: i ^ 4, odd)

    state = start_row
    for hop in range(3):
        sent = through(state, foct, foct[N:ROWS])
        got = moved(sent, lambda i: i + 8, lambda i: even(i) and i < 24)
        state = jnp.where(x == hop + 1, got, state)
    soct = compose(flag(y < 2), squad, squad_other)
    state = jnp.where(y >= 2, through(state, fquad_other, fquad_other[N:ROWS]), state)
    state = jnp.where(y % 2 == 1, through(state, fpair_other, fpair_other[N:ROWS]), state)
    sent = through(state, fmap, fmap[N:ROWS])
    got = moved(sent, lambda i: i + 1, even)
    state = jnp.where(core == 1, got, state)
    filtered, updates = forward(offsets, upwind, courant, obs_t, gains, y4, state)

    steps = (offsets, upwind, courant, smooth_gain, updates, filtered)
    own = smooth(*steps, zeros)[1]
    pair = through(own, smap_even, moved(own, lambda i: i + 1, even))
    pair_other = moved(pair, lambda i: i ^ 2, odd)
    later = y % 2 == 0
    quad = jnp.where(
        later, through(pair_other, spair, pair), through(pair, spair_other, pair_other)
    )
    quad_other = moved(quad, lambda i: i ^ 4, odd)
    oct_ = jnp.where(
        y < 2, through(quad_other, squad, quad), through(quad, squad_other, quad_other)
    )
    top = zeros
    for hop in range(3):
        sent = through(top, soct, oct_)
        got = moved(sent, lambda i: i - 8, lambda i: odd(i) and i >= 8)
        top = jnp.where(x == 2 - hop, got, top)
    top = jnp.where(y < 2, through(top, squad_other, quad_other), top)
    top = jnp.where(later, through(top, spair_other, pair_other), top)
    sent = through(top, smap, own)
    got = moved(sent, lambda i: i - 1, odd)
    top = jnp.where(core == 0, got, top)
    smoothed = smooth(*steps, top)[0]
    return filtered, smoothed


def solution(mesh):
    row = P("tm", None)
    in_specs = (P(), row, row, row, row, P("tm", None, None), row, row)
    return jax.shard_map(on_device, mesh=mesh, in_specs=in_specs, out_specs=(row, row), check_vma=False)
```

```python
import jax
import jax.numpy as jnp
from jax import lax
from jax.experimental import pallas as pl
from jax.experimental.pallas import tpu as pltpu
from jax.sharding import PartitionSpec as P

N = 512
OBS = 64
BANDS = 4
REACH = 32
DIFFUSION = 0.25
RELAXATION = 0.02
ROWS = N + 8
LANES = 128
PIECES = N // LANES
CELLS = 32
F32 = jnp.float32
BF16 = jnp.bfloat16
NT = (((1,), (1,)), ((), ()))
NN = (((1,), (0,)), ((), ()))


def lanes(rows, count=N):
    return lax.broadcasted_iota(jnp.int32, (rows, count), 1)


def pieces(v):
    return [v[:, LANES * j : LANES * (j + 1)] for j in range(PIECES)]


def ahead(parts, by):
    turn = jnp.where(by == 0, 0, LANES - by)
    turned = [pltpu.roll(part, turn, 1) for part in parts]
    here = lanes(1, LANES) + by < LANES
    return [jnp.where(here, turned[j], turned[(j + 1) % PIECES]) for j in range(PIECES)]


def neighbours(v):
    lane = lanes(1)
    left = jnp.where(lane > 0, 0.5 * DIFFUSION, 0.0)
    right = jnp.where(lane < N - 1, 0.5 * DIFFUSION, 0.0)
    return right * pltpu.roll(v, N - 1, 1) + left * pltpu.roll(v, 1, 1)


class Step:
    def __init__(self, k, offs_ref, up_ref, c_ref):
        self.offs = [offs_ref[k, band] for band in range(BANDS)]
        self.up = up_ref[pl.ds(k, 1), :]
        courant = c_ref[pl.ds(k, 1), :]
        reach = jnp.full_like(self.up, self.offs[0])
        for band in range(1, BANDS):
            reach = jnp.where(self.up == band, self.offs[band], reach)
        at = lanes(1) + reach
        inside = (at >= 0) & (at < N)
        self.centre = 1.0 - courant - DIFFUSION
        self.advected = jnp.where(inside, courant, 0.0)

    def apply(self, v):
        base = pieces(pltpu.roll(v, REACH, 1))
        ups = pieces(self.up)
        moved = ahead(base, self.offs[0] + REACH)
        for band in range(1, BANDS):
            other = ahead(base, self.offs[band] + REACH)
            moved = [jnp.where(ups[j] == band, other[j], moved[j]) for j in range(PIECES)]
        return self.centre * v + neighbours(v) + self.advected * jnp.concatenate(moved, axis=1)

    def apply_transposed(self, v):
        out = pieces(pltpu.roll(self.advected * v, REACH, 1))
        ups = pieces(pltpu.roll(self.up, REACH, 1))
        total = pieces(self.centre * v + neighbours(v))
        for band in range(BANDS):
            own = [jnp.where(ups[j] == band, out[j], 0.0) for j in range(PIECES)]
            shifted = ahead(own, REACH - self.offs[band])
            total = [total[j] + shifted[j] for j in range(PIECES)]
        return jnp.concatenate(total, axis=1)


def dot(a, b, dims=NN):
    return lax.dot_general(a, b, dims, preferred_element_type=F32)


def split2(v):
    hi = v.astype(BF16)
    return hi, (v - hi.astype(F32)).astype(BF16)


def stacked(v):
    hi = v.astype(BF16).astype(F32)
    return jnp.concatenate([hi, v - hi], axis=0).astype(BF16)


def observed_part(p, s4):
    rows = p.shape[0]
    both = dot(stacked(p), s4, NT)
    return both[:rows] + both[rows:]


def gain_rows(s, gains):
    hi, lo = split2(RELAXATION * s.astype(F32) + gains)
    return jnp.concatenate([hi, hi, lo, lo], axis=0)


def correction(e4, kk):
    hi = e4.astype(BF16).astype(F32)
    odd = (lanes(1, 4 * OBS) // OBS) % 2 == 1
    return dot(jnp.where(odd, e4 - hi, hi).astype(BF16), kk)


def one_hot(obs_row):
    own = lax.broadcasted_iota(jnp.int32, (OBS, OBS), 0) == lanes(OBS, OBS)
    column = jnp.sum(jnp.where(own, obs_row.astype(F32), 0.0), axis=1, keepdims=True)
    return jnp.where(column.astype(jnp.int32) == lanes(OBS), 1.0, 0.0).astype(BF16)


def through(v, parts_ref):
    rows = v.shape[0]
    both = stacked(v)
    high, low = dot(both, parts_ref[0], NT), dot(both, parts_ref[1], NT)
    return high[:rows] + (high[rows:] + low[:rows] + low[rows:])


def call(kernel, name, outs, operands, scratch=(), scalars=1, flops=10**8, moved=1 << 20):
    vmem, smem = pl.BlockSpec(memory_space=pltpu.VMEM), pl.BlockSpec(memory_space=pltpu.SMEM)
    return pl.pallas_call(
        kernel,
        out_shape=tuple(jax.ShapeDtypeStruct(*out) for out in outs),
        in_specs=[smem] * scalars + [vmem] * (len(operands) - scalars),
        out_specs=(vmem,) * len(outs),
        scratch_shapes=list(scratch),
        cost_estimate=pl.CostEstimate(flops=flops, bytes_accessed=moved, transcendentals=0),
        compiler_params=pltpu.CompilerParams(vmem_limit_bytes=32 << 20),
        name=name,
    )(*operands)


PARTS = ((2, N, N), BF16)
VECTOR = ((8, N), F32)


def keep_parts(values_ref, parts_ref):
    for r in range(0, N, 64):
        at = pl.ds(r, 64)
        parts_ref[0, at, :], parts_ref[1, at, :] = split2(values_ref[at, :])


def keep_columns(rows_ref, kept_ref, start):
    turned = jnp.transpose(rows_ref[...].astype(F32))
    for k in range(rows_ref.shape[0]):
        kept_ref[k, start : start + N, :] = jnp.broadcast_to(turned[:, k : k + 1], (N, LANES))


def clear_edges(padded_ref):
    edge = jnp.zeros((PIECES, REACH, LANES), F32)
    padded_ref[:, 0:REACH, :] = edge
    padded_ref[:, REACH + N : N + 2 * REACH, :] = edge


def start_identity(padded_ref):
    clear_edges(padded_ref)
    row = lax.broadcasted_iota(jnp.int32, (N, LANES), 0)
    for j in range(PIECES):
        padded_ref[j, REACH : REACH + N, :] = jnp.where(row == lanes(N, LANES) + LANES * j, 1.0, 0.0)


def keep_map(padded_ref, map_ref, parts_ref):
    for r in range(0, N, 64):
        for j in range(PIECES):
            at, cols = slice(r, r + 64), slice(LANES * j, LANES * (j + 1))
            value = padded_ref[j, REACH + r : REACH + r + 64, :]
            map_ref[at, cols] = value
            parts_ref[0, at, cols], parts_ref[1, at, cols] = split2(value)


def diffused(padded_ref, j, first, size, centre):
    at = lambda by: padded_ref[j, pl.ds(first + by, size), :]
    return centre * at(0) + (0.5 * DIFFUSION) * (at(1) + at(-1))


def filter_map(offsets, upwind, courant, obs_cells, gains, observed):
    steps = offsets.shape[0]

    def kernel(
        offs_ref, cells_ref, up_ref, c_ref, obs_ref, gains_ref, y_ref,
        map_ref, parts_ref, off_ref, s_ref, held_ref, moved_ref, picked_ref, ups_ref, cs_ref
    ):
        keep_columns(up_ref, ups_ref, 0)
        keep_columns(c_ref, cs_ref, 0)
        start_identity(held_ref)
        head = lax.broadcasted_iota(jnp.int32, (8, 1), 0) == 0

        def one(k, vec):
            step = Step(k, offs_ref, up_ref, c_ref)
            s = one_hot(obs_ref[pl.ds(k, 1), :])
            s_ref[k] = s
            gain = RELAXATION * s.astype(F32) + gains_ref[k]
            for r in range(0, N, CELLS):
                ups, cs = ups_ref[k, r : r + CELLS, :], cs_ref[k, r : r + CELLS, :]
                for j in range(PIECES):
                    at = lambda by: held_ref[j, pl.ds(REACH + r + by, CELLS), :]
                    arrived = at(step.offs[0])
                    for band in range(1, BANDS):
                        arrived = jnp.where(ups == band, at(step.offs[band]), arrived)
                    spread = diffused(held_ref, j, REACH + r, CELLS, 1.0 - cs - DIFFUSION)
                    moved_ref[j, r : r + CELLS, :] = spread + cs * arrived
            for o in range(OBS):
                for j in range(PIECES):
                    cols = slice(LANES * j, LANES * (j + 1))
                    picked_ref[o : o + 1, cols] = moved_ref[j, pl.ds(cells_ref[k, o], 1), :]
            seen_hi, seen_lo = split2(picked_ref[...])
            seen = jnp.concatenate([seen_hi, seen_lo] * 2, axis=0)
            turned = jnp.transpose(jnp.concatenate([gain, gain], axis=0))
            factors = jnp.concatenate(split2(turned), axis=1)
            for r in range(0, N, 256):
                at = slice(r, r + 256)
                corrected = pieces(dot(factors[at], seen))
                for j in range(PIECES):
                    held_ref[j, REACH + r : REACH + r + 256, :] = moved_ref[j, at, :] - corrected[j]

            high, low = split2(gain)
            kk = jnp.concatenate([high, high, low, low], axis=0)
            s4 = jnp.concatenate([s] * 4, axis=0)
            y4 = jnp.concatenate([y_ref[pl.ds(k, 1), :]] * 4, axis=1)
            p = step.apply(vec)
            return p - correction(observed_part(p, s4) - jnp.where(head, y4, 0.0), kk)

        vec = lax.fori_loop(0, steps, one, jnp.zeros((8, N), F32))
        off_ref[...] = vec
        map_ref[N:ROWS, :] = vec
        keep_map(held_ref, map_ref, parts_ref)

    return call(
        kernel,
        "filter_map",
        (((ROWS, N), F32), PARTS, VECTOR, ((steps, OBS, N), BF16)),
        (offsets, obs_cells, upwind, courant, obs_cells, gains, observed),
        scratch=[
            pltpu.VMEM((PIECES, N + 2 * REACH, LANES), F32),
            pltpu.VMEM((PIECES, N, LANES), F32),
            pltpu.VMEM((OBS, N), F32),
            pltpu.VMEM((steps, N, LANES), F32),
            pltpu.VMEM((steps, N, LANES), F32),
        ],
        scalars=2,
        flops=16 * 10**9,
        moved=4 << 20,
    )


def smoother_map(offsets, upwind, courant, smooth_gain):
    steps = offsets.shape[0]

    def kernel(offs_ref, up_ref, c_ref, sg_ref, map_ref, parts_ref, held_ref, out_ref, ups_ref, cs_ref, gains_ref):
        outside = jnp.full((REACH, LANES), -1.0, F32)
        for k in range(steps):
            ups_ref[k, 0:REACH, :] = outside
            ups_ref[k, REACH + N : N + 2 * REACH, :] = outside
        keep_columns(up_ref, ups_ref, REACH)
        keep_columns(c_ref, cs_ref, 0)
        keep_columns(sg_ref, gains_ref, 0)
        start_identity(held_ref.at[0])
        clear_edges(held_ref.at[1])
        clear_edges(out_ref)

        def one(i, carry):
            k = steps - 1 - i
            offs = [offs_ref[k, band] for band in range(BANDS)]
            now, later = held_ref.at[lax.rem(i, 2)], held_ref.at[lax.rem(i + 1, 2)]
            for r in range(0, N, CELLS):
                cs = cs_ref[k, r : r + CELLS, :]
                for j in range(PIECES):
                    at = slice(REACH + r, REACH + r + CELLS)
                    out_ref[j, at, :] = cs * now[j, at, :]
            for r in range(0, N, CELLS):
                froms = [pl.ds(REACH + r - offs[band], CELLS) for band in range(BANDS)]
                taken = [ups_ref[k, froms[band], :] == band for band in range(BANDS)]
                centre = 1.0 - cs_ref[k, r : r + CELLS, :] - DIFFUSION
                gain = gains_ref[k, r : r + CELLS, :]
                for j in range(PIECES):
                    total = diffused(now, j, REACH + r, CELLS, centre)
                    for band in range(BANDS):
                        total = total + jnp.where(taken[band], out_ref[j, froms[band], :], 0.0)
                    later[j, REACH + r : REACH + r + CELLS, :] = gain * total
            return carry

        lax.fori_loop(0, steps, one, 0)
        keep_map(held_ref.at[steps % 2], map_ref, parts_ref)

    return call(
        kernel,
        "smoother_map",
        (((N, N), F32), PARTS),
        (offsets, upwind, courant, smooth_gain),
        scratch=[
            pltpu.VMEM((2, PIECES, N + 2 * REACH, LANES), F32),
            pltpu.VMEM((PIECES, N + 2 * REACH, LANES), F32),
            pltpu.VMEM((steps, N + 2 * REACH, LANES), F32),
            pltpu.VMEM((steps, N, LANES), F32),
            pltpu.VMEM((steps, N, LANES), F32),
        ],
        flops=8 * 10**9,
        moved=2 << 20,
    )


def compose(flag, mine, other):
    rows = mine.shape[0]
    affine = rows > N

    def kernel(flag_ref, mine_ref, other_ref, out_ref, parts_ref, other_parts_ref, *offs):
        keep_parts(other_ref, other_parts_ref)
        if affine:
            offs[1][...] = other_ref[N:ROWS, :]

        def product(first_ref, second_ref):
            high, low = split2(first_ref[0:N, :])
            for start in (0, 256):
                at = pl.ds(start, 256)
                both = stacked(second_ref[at, :])
                big = dot(both, high)
                out_ref[at, :] = big[:256] + (big[256:] + dot(both[:256], low))
            if affine:
                both = stacked(first_ref[N:ROWS, :])
                keep = split2(second_ref[0:N, :])
                big, small = dot(both, keep[0], NT), dot(both, keep[1], NT)
                offset = big[:8] + (big[8:] + small[:8] + small[8:]) + second_ref[N:ROWS, :]
                out_ref[N:ROWS, :] = offset
                offs[0][...] = offset

        @pl.when(flag_ref[0] == 1)
        def _():
            product(other_ref, mine_ref)

        @pl.when(flag_ref[0] == 0)
        def _():
            product(mine_ref, other_ref)

        keep_parts(out_ref, parts_ref)

    outs = (((rows, N), F32), PARTS, PARTS) + ((VECTOR, VECTOR) if affine else ())
    return call(kernel, "compose", outs, (flag, mine, other), flops=10**9, moved=5 << 20)


def hop(place, mark, state, got, parts, offset):
    def kernel(place_ref, state_ref, got_ref, parts_ref, off_ref, new_ref, sent_ref):
        new = jnp.where(place_ref[0] == mark, got_ref[...], state_ref[...])
        new_ref[...] = new
        sent_ref[...] = through(new, parts_ref) + off_ref[...]

    return call(kernel, "hop", (VECTOR, VECTOR), (place, state, got, parts, offset))


def descend(place, mark, state, got, quad, quad_off, pair, pair_off, own, own_off):
    def kernel(place_ref, state_ref, got_ref, quad_ref, qo_ref, pair_ref, po_ref, own_ref, oo_ref, new_ref, sent_ref):
        new_ref[...] = jnp.where(place_ref[0] == mark, got_ref[...], state_ref[...])

        @pl.when(place_ref[1] == 1)
        def _():
            new_ref[...] = through(new_ref[...], quad_ref) + qo_ref[...]

        @pl.when(place_ref[2] == 1)
        def _():
            new_ref[...] = through(new_ref[...], pair_ref) + po_ref[...]

        sent_ref[...] = through(new_ref[...], own_ref) + oo_ref[...]

    operands = (place, state, got, quad, quad_off, pair, pair_off, own, own_off)
    return call(kernel, "descend", (VECTOR, VECTOR), operands)


def joined(flag, mine, other, my_parts, other_parts):
    def kernel(flag_ref, mine_ref, other_ref, mp_ref, op_ref, out_ref):
        @pl.when(flag_ref[0] == 1)
        def _():
            out_ref[...] = through(other_ref[...], mp_ref) + mine_ref[...]

        @pl.when(flag_ref[0] == 0)
        def _():
            out_ref[...] = through(mine_ref[...], op_ref) + other_ref[...]

    return call(kernel, "joined", (VECTOR,), (flag, mine, other, my_parts, other_parts))[0]


def smoothing(steps, diff, offs_ref, up_ref, c_ref, sg_ref, u_ref, store=None):
    def one(i, diff):
        k = steps - 1 - i
        step = Step(k, offs_ref, up_ref, c_ref)
        if store is not None:
            store(k, diff)
        at = pl.ds(k, 1)
        return sg_ref[at, :] * step.apply_transposed(diff + u_ref[at, :])

    return lax.fori_loop(0, steps, one, diff)


def forward(place, offsets, upwind, courant, smooth_gain, hots, gains, observed, state, got):
    steps = offsets.shape[0]

    def kernel(
        place_ref, offs_ref, up_ref, c_ref, sg_ref, s_ref, gains_ref, y_ref, state_ref, got_ref, filt_ref, upd_ref, end_ref
    ):
        first = lax.broadcasted_iota(jnp.int32, (8, 1), 0) == 0

        def one(k, vec):
            step = Step(k, offs_ref, up_ref, c_ref)
            s = s_ref[k]
            kk = gain_rows(s, gains_ref[k])
            s4 = jnp.concatenate([s] * 4, axis=0)
            y4 = jnp.concatenate([y_ref[pl.ds(k, 1), :]] * 4, axis=1)
            p = step.apply(vec)
            update = -correction(observed_part(p, s4) - jnp.where(first, y4, 0.0), kk)
            vec = p + update
            filt_ref[pl.ds(k, 1), :] = vec[0:1]
            upd_ref[pl.ds(k, 1), :] = update[0:1]
            return vec

        start = jnp.where(place_ref[0] == 1, got_ref[...], state_ref[...])
        lax.fori_loop(0, steps, one, start)
        zeros = jnp.zeros((8, N), F32)
        end_ref[...] = smoothing(steps, zeros, offs_ref, up_ref, c_ref, sg_ref, upd_ref)

    return call(
        kernel,
        "forward",
        (((steps, N), F32), ((steps, N), F32), VECTOR),
        (place, offsets, upwind, courant, smooth_gain, hots, gains, observed, state, got),
        scalars=2,
        flops=4 * 10**9,
        moved=3 << 20,
    )


def smooth(place, offsets, upwind, courant, smooth_gain, updates, filtered, top, got):
    steps = offsets.shape[0]

    def kernel(place_ref, offs_ref, up_ref, c_ref, sg_ref, u_ref, x_ref, top_ref, got_ref, out_ref):
        def store(k, diff):
            at = pl.ds(k, 1)
            out_ref[at, :] = x_ref[at, :] + diff[0:1]

        diff = jnp.where(place_ref[0] == 0, got_ref[...], top_ref[...])
        smoothing(steps, diff, offs_ref, up_ref, c_ref, sg_ref, u_ref, store)

    return call(
        kernel,
        "smooth",
        (((steps, N), F32),),
        (place, offsets, upwind, courant, smooth_gain, updates, filtered, top, got),
        scalars=2,
    )[0]


def on_device(initial, offsets, upwind, courant, obs_cells, gains, observed, smooth_gain):
    place = lax.axis_index("tm")
    x, y, core = place // 8, (place // 2) % 4, place % 2

    def moved(values, to, senders):
        return lax.ppermute(values, "tm", [(i, to(i)) for i in range(32) if senders(i)])

    even = lambda i: i % 2 == 0
    odd = lambda i: i % 2 == 1
    ints = lambda *values: jnp.stack([jnp.asarray(v, jnp.int32) for v in values])
    never = jnp.zeros((1,), jnp.int32)
    at_core = ints(core)
    y_odd, y_even, y_high, y_low = ints(y % 2 == 1), ints(y % 2 == 0), ints(y >= 2), ints(y < 2)
    start_row = jnp.broadcast_to(initial[None, :], (8, N))
    zeros = jnp.zeros((8, N), F32)

    fmap, fmap_p, fmap_o, hots = filter_map(offsets, upwind, courant, obs_cells, gains, observed)
    fmap_odd = moved(fmap, lambda i: i - 1, odd)
    fpair, fpair_p, _, _, _ = compose(never, fmap, fmap_odd)
    fpair_other = moved(fpair, lambda i: i ^ 2, even)
    smap, smap_p = smoother_map(offsets, upwind, courant, smooth_gain)
    smap_even = moved(smap, lambda i: i + 1, even)
    fquad, fquad_p, fpair_op, _, fpair_oo = compose(y_odd, fpair, fpair_other)
    fquad_other = moved(fquad, lambda i: i ^ 4, even)
    spair, spair_p, smap_ep = compose(never, smap, smap_even)
    spair_other = moved(spair, lambda i: i ^ 2, odd)
    foct, foct_p, fquad_op, foct_o, fquad_oo = compose(y_high, fquad, fquad_other)

    place3 = ints(x, y >= 2, y % 2 == 1)
    ahead_of = lambda v: moved(v, lambda i: i + 8, lambda i: even(i) and i < 24)
    state, sent = hop(place3, 0, start_row, start_row, foct_p, foct_o)
    got = ahead_of(sent)
    squad, squad_p, spair_op = compose(y_even, spair, spair_other)
    squad_other = moved(squad, lambda i: i ^ 4, odd)
    state, sent = hop(place3, 1, state, got, foct_p, foct_o)
    got = ahead_of(sent)
    state, sent = hop(place3, 2, state, got, foct_p, foct_o)
    got = ahead_of(sent)
    state, sent = descend(
        place3, 3, state, got, fquad_op, fquad_oo, fpair_op, fpair_oo, fmap_p, fmap_o
    )
    got = moved(sent, lambda i: i + 1, even)
    _, soct_p, squad_op = compose(y_low, squad, squad_other)
    filtered, updates, own = forward(
        at_core, offsets, upwind, courant, smooth_gain, hots, gains, observed, state, got
    )

    pair = joined(never, own, moved(own, lambda i: i + 1, even), smap_p, smap_ep)
    pair_other = moved(pair, lambda i: i ^ 2, odd)
    quad = joined(y_even, pair, pair_other, spair_p, spair_op)
    quad_other = moved(quad, lambda i: i ^ 4, odd)
    octet = joined(y_low, quad, quad_other, squad_p, squad_op)
    place3 = ints(x, y < 2, y % 2 == 0)
    behind = lambda v: moved(v, lambda i: i - 8, lambda i: odd(i) and i >= 8)
    got = behind(octet)
    top, sent = hop(place3, 2, zeros, got, soct_p, octet)
    got = behind(sent)
    top, sent = hop(place3, 1, top, got, soct_p, octet)
    got = behind(sent)
    top, sent = descend(place3, 0, top, got, squad_op, quad_other, spair_op, pair_other, smap_p, own)
    got = moved(sent, lambda i: i - 1, odd)
    smoothed = smooth(
        at_core, offsets, upwind, courant, smooth_gain, updates, filtered, top, got
    )
    return filtered, smoothed


def solution(mesh):
    row = P("tm", None)
    in_specs = (P(), row, row, row, row, P("tm", None, None), row, row)
    return jax.shard_map(on_device, mesh=mesh, in_specs=in_specs, out_specs=(row, row), check_vma=False)
```

```python
import jax
import jax.numpy as jnp
from jax import lax
from jax.experimental import pallas as pl
from jax.experimental.pallas import tpu as pltpu
from jax.sharding import PartitionSpec as P

N = 512
OBS = 64
BANDS = 4
REACH = 32
DIFFUSION = 0.25
RELAXATION = 0.02
ROWS = N + 8
LANES = 128
PIECES = N // LANES
CELLS = 32
F32 = jnp.float32
BF16 = jnp.bfloat16
NT = (((1,), (1,)), ((), ()))
NN = (((1,), (0,)), ((), ()))


def lanes(rows, count=N):
    return lax.broadcasted_iota(jnp.int32, (rows, count), 1)


def pieces(v):
    return [v[:, LANES * j : LANES * (j + 1)] for j in range(PIECES)]


def ahead(parts, by):
    turn = jnp.where(by == 0, 0, LANES - by)
    turned = [pltpu.roll(part, turn, 1) for part in parts]
    here = lanes(1, LANES) + by < LANES
    return [jnp.where(here, turned[j], turned[(j + 1) % PIECES]) for j in range(PIECES)]


def neighbours(v):
    lane = lanes(1)
    left = jnp.where(lane > 0, 0.5 * DIFFUSION, 0.0)
    right = jnp.where(lane < N - 1, 0.5 * DIFFUSION, 0.0)
    return right * pltpu.roll(v, N - 1, 1) + left * pltpu.roll(v, 1, 1)


class Step:
    def __init__(self, k, offs_ref, up_ref, c_ref):
        self.offs = [offs_ref[k, band] for band in range(BANDS)]
        self.up = up_ref[pl.ds(k, 1), :]
        courant = c_ref[pl.ds(k, 1), :]
        reach = jnp.full_like(self.up, self.offs[0])
        for band in range(1, BANDS):
            reach = jnp.where(self.up == band, self.offs[band], reach)
        at = lanes(1) + reach
        inside = (at >= 0) & (at < N)
        self.centre = 1.0 - courant - DIFFUSION
        self.advected = jnp.where(inside, courant, 0.0)

    def apply(self, v):
        base = pieces(pltpu.roll(v, REACH, 1))
        ups = pieces(self.up)
        moved = ahead(base, self.offs[0] + REACH)
        for band in range(1, BANDS):
            other = ahead(base, self.offs[band] + REACH)
            moved = [jnp.where(ups[j] == band, other[j], moved[j]) for j in range(PIECES)]
        return self.centre * v + neighbours(v) + self.advected * jnp.concatenate(moved, axis=1)

    def apply_transposed(self, v):
        out = pieces(pltpu.roll(self.advected * v, REACH, 1))
        ups = pieces(pltpu.roll(self.up, REACH, 1))
        total = pieces(self.centre * v + neighbours(v))
        for band in range(BANDS):
            own = [jnp.where(ups[j] == band, out[j], 0.0) for j in range(PIECES)]
            shifted = ahead(own, REACH - self.offs[band])
            total = [total[j] + shifted[j] for j in range(PIECES)]
        return jnp.concatenate(total, axis=1)


def dot(a, b, dims=NN):
    return lax.dot_general(a, b, dims, preferred_element_type=F32)


def split2(v):
    hi = v.astype(BF16)
    return hi, (v - hi.astype(F32)).astype(BF16)


def stacked(v):
    hi = v.astype(BF16).astype(F32)
    return jnp.concatenate([hi, v - hi], axis=0).astype(BF16)


def observed_part(p, s4):
    rows = p.shape[0]
    both = dot(stacked(p), s4, NT)
    return both[:rows] + both[rows:]


def gain_rows(s, gains):
    hi, lo = split2(RELAXATION * s.astype(F32) + gains)
    return jnp.concatenate([hi, hi, lo, lo], axis=0)


def correction(e4, kk):
    hi = e4.astype(BF16).astype(F32)
    odd = (lanes(1, 4 * OBS) // OBS) % 2 == 1
    return dot(jnp.where(odd, e4 - hi, hi).astype(BF16), kk)


def one_hot(obs_row):
    own = lax.broadcasted_iota(jnp.int32, (OBS, OBS), 0) == lanes(OBS, OBS)
    column = jnp.sum(jnp.where(own, obs_row.astype(F32), 0.0), axis=1, keepdims=True)
    return jnp.where(column.astype(jnp.int32) == lanes(OBS), 1.0, 0.0).astype(BF16)


def through(v, parts_ref):
    rows = v.shape[0]
    both = stacked(v)
    high, low = dot(both, parts_ref[0], NT), dot(both, parts_ref[1], NT)
    return high[:rows] + (high[rows:] + low[:rows] + low[rows:])


def call(kernel, name, outs, operands, scratch=(), scalars=1, far=0, flops=10**8, moved=1 << 20, limit=16):
    vmem, smem = pl.BlockSpec(memory_space=pltpu.VMEM), pl.BlockSpec(memory_space=pltpu.SMEM)
    anywhere = pl.BlockSpec(memory_space=pltpu.MemorySpace.HBM)
    near_hbm = [
        pltpu.with_memory_space_constraint(value, pltpu.MemorySpace.HBM)
        for value in operands[scalars : scalars + far]
    ]
    return pl.pallas_call(
        kernel,
        out_shape=tuple(jax.ShapeDtypeStruct(*out) for out in outs),
        in_specs=[smem] * scalars + [anywhere] * far + [vmem] * (len(operands) - scalars - far),
        out_specs=(vmem,) * len(outs),
        scratch_shapes=list(scratch),
        cost_estimate=pl.CostEstimate(flops=flops, bytes_accessed=moved, transcendentals=0),
        compiler_params=pltpu.CompilerParams(vmem_limit_bytes=limit << 20),
        name=name,
    )(*operands[:scalars], *near_hbm, *operands[scalars + far :])


PARTS = ((2, N, N), BF16)
VECTOR = ((8, N), F32)


def keep_parts(values_ref, parts_ref):
    for r in range(0, N, 64):
        at = pl.ds(r, 64)
        parts_ref[0, at, :], parts_ref[1, at, :] = split2(values_ref[at, :])


def keep_columns(rows_ref, kept_ref, start):
    turned = jnp.transpose(rows_ref[...].astype(F32))
    for k in range(rows_ref.shape[0]):
        kept_ref[k, start : start + N, :] = jnp.broadcast_to(turned[:, k : k + 1], (N, LANES))


def clear_edges(padded_ref):
    edge = jnp.zeros((PIECES, REACH, LANES), F32)
    padded_ref[:, 0:REACH, :] = edge
    padded_ref[:, REACH + N : N + 2 * REACH, :] = edge


def start_identity(padded_ref):
    clear_edges(padded_ref)
    row = lax.broadcasted_iota(jnp.int32, (N, LANES), 0)
    for j in range(PIECES):
        padded_ref[j, REACH : REACH + N, :] = jnp.where(row == lanes(N, LANES) + LANES * j, 1.0, 0.0)


def keep_map(padded_ref, map_ref, parts_ref):
    for r in range(0, N, 64):
        for j in range(PIECES):
            at, cols = slice(r, r + 64), slice(LANES * j, LANES * (j + 1))
            value = padded_ref[j, REACH + r : REACH + r + 64, :]
            map_ref[at, cols] = value
            parts_ref[0, at, cols], parts_ref[1, at, cols] = split2(value)


def diffused(padded_ref, j, first, size, centre):
    at = lambda by: padded_ref[j, pl.ds(first + by, size), :]
    return centre * at(0) + (0.5 * DIFFUSION) * (at(1) + at(-1))


def filter_map(offsets, upwind, courant, obs_cells, gains, observed):
    steps = offsets.shape[0]

    def kernel(
        offs_ref, cells_ref, up_far, c_far, obs_far, y_far, gains_far,
        map_ref, parts_ref, off_ref, s_ref, held_ref, moved_ref, picked_ref, ups_ref, cs_ref,
        up_ref, c_ref, obs_ref, y_ref, gains_ref, sem
    ):
        pairs = ((up_far, up_ref), (c_far, c_ref), (obs_far, obs_ref), (y_far, y_ref))
        copies = [pltpu.make_async_copy(a, b, sem.at[i]) for i, (a, b) in enumerate(pairs)]
        for copy in copies:
            copy.start()
        fetch = lambda k: pltpu.make_async_copy(gains_far.at[k], gains_ref.at[k], sem.at[4 + k])
        for k in range(steps):
            fetch(k).start()
        start_identity(held_ref)
        for copy in copies:
            copy.wait()
        keep_columns(up_ref, ups_ref, 0)
        keep_columns(c_ref, cs_ref, 0)
        head = lax.broadcasted_iota(jnp.int32, (8, 1), 0) == 0

        def one(k, vec):
            step = Step(k, offs_ref, up_ref, c_ref)
            s = one_hot(obs_ref[pl.ds(k, 1), :])
            s_ref[k] = s
            fetch(k).wait()
            gain = RELAXATION * s.astype(F32) + gains_ref[k]
            for r in range(0, N, CELLS):
                ups, cs = ups_ref[k, r : r + CELLS, :], cs_ref[k, r : r + CELLS, :]
                for j in range(PIECES):
                    at = lambda by: held_ref[j, pl.ds(REACH + r + by, CELLS), :]
                    arrived = at(step.offs[0])
                    for band in range(1, BANDS):
                        arrived = jnp.where(ups == band, at(step.offs[band]), arrived)
                    spread = diffused(held_ref, j, REACH + r, CELLS, 1.0 - cs - DIFFUSION)
                    moved_ref[j, r : r + CELLS, :] = spread + cs * arrived
            for o in range(OBS):
                for j in range(PIECES):
                    cols = slice(LANES * j, LANES * (j + 1))
                    picked_ref[o : o + 1, cols] = moved_ref[j, pl.ds(cells_ref[k, o], 1), :]
            seen_hi, seen_lo = split2(picked_ref[...])
            seen = jnp.concatenate([seen_hi, seen_lo] * 2, axis=0)
            turned = jnp.transpose(jnp.concatenate([gain, gain], axis=0))
            factors = jnp.concatenate(split2(turned), axis=1)
            for r in range(0, N, 256):
                at = slice(r, r + 256)
                corrected = pieces(dot(factors[at], seen))
                for j in range(PIECES):
                    held_ref[j, REACH + r : REACH + r + 256, :] = moved_ref[j, at, :] - corrected[j]

            high, low = split2(gain)
            kk = jnp.concatenate([high, high, low, low], axis=0)
            s4 = jnp.concatenate([s] * 4, axis=0)
            y4 = jnp.concatenate([y_ref[pl.ds(k, 1), :]] * 4, axis=1)
            p = step.apply(vec)
            return p - correction(observed_part(p, s4) - jnp.where(head, y4, 0.0), kk)

        vec = lax.fori_loop(0, steps, one, jnp.zeros((8, N), F32))
        off_ref[...] = vec
        map_ref[N:ROWS, :] = vec
        keep_map(held_ref, map_ref, parts_ref)

    return call(
        kernel,
        "filter_map",
        (((ROWS, N), F32), PARTS, VECTOR, ((steps, OBS, N), BF16)),
        (offsets, obs_cells, upwind, courant, obs_cells, observed, gains),
        scratch=[
            pltpu.VMEM((PIECES, N + 2 * REACH, LANES), F32),
            pltpu.VMEM((PIECES, N, LANES), F32),
            pltpu.VMEM((OBS, N), F32),
            pltpu.VMEM((steps, N, LANES), F32),
            pltpu.VMEM((steps, N, LANES), F32),
            pltpu.VMEM((steps, N), jnp.int32),
            pltpu.VMEM((steps, N), F32),
            pltpu.VMEM((steps, OBS), jnp.int32),
            pltpu.VMEM((steps, OBS), F32),
            pltpu.VMEM((steps, OBS, N), F32),
            pltpu.SemaphoreType.DMA((4 + steps,)),
        ],
        scalars=2,
        far=5,
        flops=16 * 10**9,
        moved=4 << 20,
        limit=28,
    )


def smoother_map(offsets, upwind, courant, smooth_gain):
    steps = offsets.shape[0]

    def kernel(offs_ref, up_ref, c_ref, sg_ref, map_ref, parts_ref, held_ref, out_ref, ups_ref, cs_ref, gains_ref):
        outside = jnp.full((REACH, LANES), -1.0, F32)
        for k in range(steps):
            ups_ref[k, 0:REACH, :] = outside
            ups_ref[k, REACH + N : N + 2 * REACH, :] = outside
        keep_columns(up_ref, ups_ref, REACH)
        keep_columns(c_ref, cs_ref, 0)
        keep_columns(sg_ref, gains_ref, 0)
        start_identity(held_ref.at[0])
        clear_edges(held_ref.at[1])
        clear_edges(out_ref)

        def one(i, carry):
            k = steps - 1 - i
            offs = [offs_ref[k, band] for band in range(BANDS)]
            now, later = held_ref.at[lax.rem(i, 2)], held_ref.at[lax.rem(i + 1, 2)]
            for r in range(0, N, CELLS):
                cs = cs_ref[k, r : r + CELLS, :]
                for j in range(PIECES):
                    at = slice(REACH + r, REACH + r + CELLS)
                    out_ref[j, at, :] = cs * now[j, at, :]
            for r in range(0, N, CELLS):
                froms = [pl.ds(REACH + r - offs[band], CELLS) for band in range(BANDS)]
                taken = [ups_ref[k, froms[band], :] == band for band in range(BANDS)]
                centre = 1.0 - cs_ref[k, r : r + CELLS, :] - DIFFUSION
                gain = gains_ref[k, r : r + CELLS, :]
                for j in range(PIECES):
                    total = diffused(now, j, REACH + r, CELLS, centre)
                    for band in range(BANDS):
                        total = total + jnp.where(taken[band], out_ref[j, froms[band], :], 0.0)
                    later[j, REACH + r : REACH + r + CELLS, :] = gain * total
            return carry

        lax.fori_loop(0, steps, one, 0)
        keep_map(held_ref.at[steps % 2], map_ref, parts_ref)

    return call(
        kernel,
        "smoother_map",
        (((N, N), F32), PARTS),
        (offsets, upwind, courant, smooth_gain),
        scratch=[
            pltpu.VMEM((2, PIECES, N + 2 * REACH, LANES), F32),
            pltpu.VMEM((PIECES, N + 2 * REACH, LANES), F32),
            pltpu.VMEM((steps, N + 2 * REACH, LANES), F32),
            pltpu.VMEM((steps, N, LANES), F32),
            pltpu.VMEM((steps, N, LANES), F32),
        ],
        flops=8 * 10**9,
        moved=2 << 20,
        limit=28,
    )


def compose(flag, mine, other, keep=True, parts=False, other_parts=False):
    rows = mine.shape[0]
    affine = rows > N
    kinds = (("out", keep, ((rows, N), F32)), ("off", affine, VECTOR), ("parts", parts, PARTS), ("other", other_parts, PARTS))

    def kernel(flag_ref, mine_ref, other_ref, *out_refs):
        refs = dict(zip([name for name, wanted, _ in kinds if wanted], out_refs, strict=True))

        def product(first_ref, second_ref):
            if other_parts:
                keep_parts(other_ref, refs["other"])
            high, low = split2(first_ref[0:N, :])
            for start in (0, 256):
                at = pl.ds(start, 256)
                both = stacked(second_ref[at, :])
                big = dot(both, high)
                total = big[:256] + (big[256:] + dot(both[:256], low))
                if keep:
                    refs["out"][at, :] = total
                if parts:
                    refs["parts"][0, at, :], refs["parts"][1, at, :] = split2(total)
            if affine:
                both = stacked(first_ref[N:ROWS, :])
                halves = split2(second_ref[0:N, :])
                big, small = dot(both, halves[0], NT), dot(both, halves[1], NT)
                offset = big[:8] + (big[8:] + small[:8] + small[8:]) + second_ref[N:ROWS, :]
                refs["off"][...] = offset
                if keep:
                    refs["out"][N:ROWS, :] = offset

        @pl.when(flag_ref[0] == 1)
        def _():
            product(other_ref, mine_ref)

        @pl.when(flag_ref[0] == 0)
        def _():
            product(mine_ref, other_ref)

    outs = tuple(shape for _, wanted, shape in kinds if wanted)
    return call(kernel, "compose", outs, (flag, mine, other), flops=10**9, moved=5 << 20)


def parted(maps):
    def kernel(map_ref, parts_ref, off_ref):
        keep_parts(map_ref, parts_ref)
        off_ref[...] = map_ref[N:ROWS, :]

    return call(kernel, "parted", (PARTS, VECTOR), (maps,), scalars=0, flops=10**8, moved=2 << 20)


def hop(place, mark, state, got, parts, offset):
    def kernel(place_ref, state_ref, got_ref, parts_ref, off_ref, new_ref, sent_ref):
        new = jnp.where(place_ref[0] == mark, got_ref[...], state_ref[...])
        new_ref[...] = new
        sent_ref[...] = through(new, parts_ref) + off_ref[...]

    return call(kernel, "hop", (VECTOR, VECTOR), (place, state, got, parts, offset))


def descend(place, mark, state, got, quad, quad_off, pair, pair_off, own, own_off):
    def kernel(place_ref, state_ref, got_ref, quad_ref, qo_ref, pair_ref, po_ref, own_ref, oo_ref, new_ref, sent_ref):
        new_ref[...] = jnp.where(place_ref[0] == mark, got_ref[...], state_ref[...])

        @pl.when(place_ref[1] == 1)
        def _():
            new_ref[...] = through(new_ref[...], quad_ref) + qo_ref[...]

        @pl.when(place_ref[2] == 1)
        def _():
            new_ref[...] = through(new_ref[...], pair_ref) + po_ref[...]

        sent_ref[...] = through(new_ref[...], own_ref) + oo_ref[...]

    operands = (place, state, got, quad, quad_off, pair, pair_off, own, own_off)
    return call(kernel, "descend", (VECTOR, VECTOR), operands)


def joined(flag, mine, other, my_parts, other_parts):
    def kernel(flag_ref, mine_ref, other_ref, mp_ref, op_ref, out_ref):
        @pl.when(flag_ref[0] == 1)
        def _():
            out_ref[...] = through(other_ref[...], mp_ref) + mine_ref[...]

        @pl.when(flag_ref[0] == 0)
        def _():
            out_ref[...] = through(mine_ref[...], op_ref) + other_ref[...]

    return call(kernel, "joined", (VECTOR,), (flag, mine, other, my_parts, other_parts))[0]


def smoothing(steps, diff, offs_ref, up_ref, c_ref, sg_ref, u_ref, store=None):
    def one(i, diff):
        k = steps - 1 - i
        step = Step(k, offs_ref, up_ref, c_ref)
        if store is not None:
            store(k, diff)
        at = pl.ds(k, 1)
        return sg_ref[at, :] * step.apply_transposed(diff + u_ref[at, :])

    return lax.fori_loop(0, steps, one, diff)


def forward(place, offsets, upwind, courant, smooth_gain, hots, gains, observed, state, got):
    steps = offsets.shape[0]

    def kernel(
        place_ref, offs_ref, s_far, gains_far, up_ref, c_ref, sg_ref, y_ref, state_ref, got_ref,
        filt_ref, upd_ref, end_ref, s_ref, gains_ref, sem
    ):
        def fetch(k):
            return (
                pltpu.make_async_copy(s_far.at[k], s_ref.at[k], sem.at[k]),
                pltpu.make_async_copy(gains_far.at[k], gains_ref.at[k], sem.at[steps + k]),
            )

        for k in range(steps):
            for copy in fetch(k):
                copy.start()
        first = lax.broadcasted_iota(jnp.int32, (8, 1), 0) == 0

        def one(k, vec):
            step = Step(k, offs_ref, up_ref, c_ref)
            for copy in fetch(k):
                copy.wait()
            s = s_ref[k]
            kk = gain_rows(s, gains_ref[k])
            s4 = jnp.concatenate([s] * 4, axis=0)
            y4 = jnp.concatenate([y_ref[pl.ds(k, 1), :]] * 4, axis=1)
            p = step.apply(vec)
            update = -correction(observed_part(p, s4) - jnp.where(first, y4, 0.0), kk)
            vec = p + update
            filt_ref[pl.ds(k, 1), :] = vec[0:1]
            upd_ref[pl.ds(k, 1), :] = update[0:1]
            return vec

        start = jnp.where(place_ref[0] == 1, got_ref[...], state_ref[...])
        lax.fori_loop(0, steps, one, start)
        zeros = jnp.zeros((8, N), F32)
        end_ref[...] = smoothing(steps, zeros, offs_ref, up_ref, c_ref, sg_ref, upd_ref)

    return call(
        kernel,
        "forward",
        (((steps, N), F32), ((steps, N), F32), VECTOR),
        (place, offsets, hots, gains, upwind, courant, smooth_gain, observed, state, got),
        scratch=[
            pltpu.VMEM((steps, OBS, N), BF16),
            pltpu.VMEM((steps, OBS, N), F32),
            pltpu.SemaphoreType.DMA((2 * steps,)),
        ],
        scalars=2,
        far=2,
        flops=4 * 10**9,
        moved=3 << 20,
    )


def smooth(place, offsets, upwind, courant, smooth_gain, updates, filtered, top, got):
    steps = offsets.shape[0]

    def kernel(place_ref, offs_ref, up_ref, c_ref, sg_ref, u_ref, x_ref, top_ref, got_ref, out_ref):
        def store(k, diff):
            at = pl.ds(k, 1)
            out_ref[at, :] = x_ref[at, :] + diff[0:1]

        diff = jnp.where(place_ref[0] == 0, got_ref[...], top_ref[...])
        smoothing(steps, diff, offs_ref, up_ref, c_ref, sg_ref, u_ref, store)

    return call(
        kernel,
        "smooth",
        (((steps, N), F32),),
        (place, offsets, upwind, courant, smooth_gain, updates, filtered, top, got),
        scalars=2,
    )[0]


def on_device(initial, offsets, upwind, courant, obs_cells, gains, observed, smooth_gain):
    place = lax.axis_index("tm")
    x, y, core = place // 8, (place // 2) % 4, place % 2

    def moved(values, to, senders):
        return lax.ppermute(values, "tm", [(i, to(i)) for i in range(32) if senders(i)])

    even = lambda i: i % 2 == 0
    odd = lambda i: i % 2 == 1
    ints = lambda *values: jnp.stack([jnp.asarray(v, jnp.int32) for v in values])
    never = jnp.zeros((1,), jnp.int32)
    at_core = ints(core)
    on_even = lambda flag: ints(jnp.where(core == 0, flag, 2))
    on_odd = lambda flag: ints(jnp.where(core == 1, flag, 2))
    y_even, y_low = ints(y % 2 == 0), ints(y < 2)
    start_row = jnp.broadcast_to(initial[None, :], (8, N))
    zeros = jnp.zeros((8, N), F32)

    after = lambda value, *before: lax.optimization_barrier((value, *before))[0]

    fmap, fmap_p, fmap_o, hots = filter_map(offsets, upwind, courant, obs_cells, gains, observed)
    fmap_odd = moved(fmap, lambda i: i - 1, odd)
    fpair, fpair_o = compose(on_even(0), fmap, fmap_odd)
    fpair_other = moved(fpair, lambda i: i ^ 2, even)
    smap, smap_p = smoother_map(offsets, after(upwind, fpair_o), courant, smooth_gain)
    smap_even = moved(smap, lambda i: i + 1, even)
    fquad, fquad_o = compose(on_even(y % 2), fpair, fpair_other)
    fquad_other = moved(fquad, lambda i: i ^ 4, even)
    smap_even = after(smap_even, fquad_o)
    spair, spair_p, smap_ep = compose(on_odd(0), smap, smap_even, parts=True, other_parts=True)
    fpair_op, fpair_oo = parted(fpair_other)
    foct_o, foct_p = compose(on_even(y // 2), fquad, fquad_other, keep=False, parts=True)
    spair_other = moved(after(spair, foct_o), lambda i: i ^ 2, odd)

    place3 = ints(x, y >= 2, y % 2 == 1)
    ahead_of = lambda v: moved(v, lambda i: i + 8, lambda i: even(i) and i < 24)
    state, sent = hop(place3, 0, start_row, start_row, foct_p, foct_o)
    got = ahead_of(sent)
    fquad_op, fquad_oo = parted(fquad_other)
    state, sent = hop(place3, 1, after(state, fquad_oo), got, foct_p, foct_o)
    got = ahead_of(sent)
    state, sent = hop(place3, 2, state, got, foct_p, foct_o)
    got = ahead_of(sent)
    squad, squad_p, spair_op = compose(
        on_odd(1 - y % 2), spair, after(spair_other, sent), parts=True, other_parts=True
    )
    squad_other = moved(squad, lambda i: i ^ 4, odd)
    state, sent = descend(
        place3, 3, after(state, squad_p), got, fquad_op, fquad_oo, fpair_op, fpair_oo, fmap_p, fmap_o
    )
    got = moved(sent, lambda i: i + 1, even)
    filtered, updates, own = forward(
        at_core, offsets, upwind, courant, smooth_gain, hots, gains, observed, state, got
    )
    soct_p, squad_op = compose(
        on_odd(1 - y // 2), squad, after(squad_other, own), keep=False, parts=True, other_parts=True
    )

    pair = joined(never, own, moved(own, lambda i: i + 1, even), smap_p, smap_ep)
    pair_other = moved(pair, lambda i: i ^ 2, odd)
    quad = joined(y_even, pair, pair_other, spair_p, spair_op)
    quad_other = moved(quad, lambda i: i ^ 4, odd)
    octet = joined(y_low, quad, quad_other, squad_p, squad_op)
    place3 = ints(x, y < 2, y % 2 == 0)
    behind = lambda v: moved(v, lambda i: i - 8, lambda i: odd(i) and i >= 8)
    got = behind(octet)
    top, sent = hop(place3, 2, zeros, got, soct_p, octet)
    got = behind(sent)
    top, sent = hop(place3, 1, top, got, soct_p, octet)
    got = behind(sent)
    top, sent = descend(place3, 0, top, got, squad_op, quad_other, spair_op, pair_other, smap_p, own)
    got = moved(sent, lambda i: i - 1, odd)
    smoothed = smooth(
        at_core, offsets, upwind, courant, smooth_gain, updates, filtered, top, got
    )
    return filtered, smoothed


def solution(mesh):
    row = P("tm", None)
    in_specs = (P(), row, row, row, row, P("tm", None, None), row, row)
    return jax.shard_map(on_device, mesh=mesh, in_specs=in_specs, out_specs=(row, row), check_vma=False)
```

```python
import jax
import jax.numpy as jnp
from jax import lax
from jax.experimental import pallas as pl
from jax.experimental.pallas import tpu as pltpu
from jax.sharding import PartitionSpec as P

N = 512
OBS = 64
BANDS = 4
REACH = 32
DIFFUSION = 0.25
RELAXATION = 0.02
ROWS = N + 8
LANES = 128
PIECES = N // LANES
CELLS = 32
F32 = jnp.float32
BF16 = jnp.bfloat16
NT = (((1,), (1,)), ((), ()))
NN = (((1,), (0,)), ((), ()))


def lanes(rows, count=N):
    return lax.broadcasted_iota(jnp.int32, (rows, count), 1)


def pieces(v):
    return [v[:, LANES * j : LANES * (j + 1)] for j in range(PIECES)]


def ahead(parts, by):
    turn = jnp.where(by == 0, 0, LANES - by)
    turned = [pltpu.roll(part, turn, 1) for part in parts]
    here = lanes(1, LANES) + by < LANES
    return [jnp.where(here, turned[j], turned[(j + 1) % PIECES]) for j in range(PIECES)]


def neighbours(v):
    lane = lanes(1)
    left = jnp.where(lane > 0, 0.5 * DIFFUSION, 0.0)
    right = jnp.where(lane < N - 1, 0.5 * DIFFUSION, 0.0)
    return right * pltpu.roll(v, N - 1, 1) + left * pltpu.roll(v, 1, 1)


class Step:
    def __init__(self, k, offs_ref, up_ref, c_ref):
        self.offs = [offs_ref[k, band] for band in range(BANDS)]
        self.up = up_ref[pl.ds(k, 1), :]
        courant = c_ref[pl.ds(k, 1), :]
        reach = jnp.full_like(self.up, self.offs[0])
        for band in range(1, BANDS):
            reach = jnp.where(self.up == band, self.offs[band], reach)
        at = lanes(1) + reach
        inside = (at >= 0) & (at < N)
        self.centre = 1.0 - courant - DIFFUSION
        self.advected = jnp.where(inside, courant, 0.0)

    def apply(self, v):
        base = pieces(pltpu.roll(v, REACH, 1))
        ups = pieces(self.up)
        moved = ahead(base, self.offs[0] + REACH)
        for band in range(1, BANDS):
            other = ahead(base, self.offs[band] + REACH)
            moved = [jnp.where(ups[j] == band, other[j], moved[j]) for j in range(PIECES)]
        return self.centre * v + neighbours(v) + self.advected * jnp.concatenate(moved, axis=1)

    def apply_transposed(self, v):
        out = pieces(pltpu.roll(self.advected * v, REACH, 1))
        ups = pieces(pltpu.roll(self.up, REACH, 1))
        total = pieces(self.centre * v + neighbours(v))
        for band in range(BANDS):
            own = [jnp.where(ups[j] == band, out[j], 0.0) for j in range(PIECES)]
            shifted = ahead(own, REACH - self.offs[band])
            total = [total[j] + shifted[j] for j in range(PIECES)]
        return jnp.concatenate(total, axis=1)


def dot(a, b, dims=NN):
    return lax.dot_general(a, b, dims, preferred_element_type=F32)


def split2(v):
    hi = v.astype(BF16)
    return hi, (v - hi.astype(F32)).astype(BF16)


def stacked(v):
    hi = v.astype(BF16).astype(F32)
    return jnp.concatenate([hi, v - hi], axis=0).astype(BF16)


def observed_part(p, s2):
    rows = p.shape[0]
    both = dot(stacked(p), s2, NT)
    return both[:rows] + both[rows:]


def gain_rows(s, gains):
    hi, lo = split2(RELAXATION * s.astype(F32) + gains)
    return jnp.concatenate([hi, hi, lo, lo], axis=0)


def correction(e2, kk):
    hi = e2.astype(BF16).astype(F32)
    mixed = jnp.where(lanes(1, 2 * OBS) >= OBS, e2 - hi, hi)
    return dot(jnp.concatenate([mixed, mixed], axis=1).astype(BF16), kk)


def one_hot(obs_row):
    own = lax.broadcasted_iota(jnp.int32, (OBS, OBS), 0) == lanes(OBS, OBS)
    column = jnp.sum(jnp.where(own, obs_row.astype(F32), 0.0), axis=1, keepdims=True)
    return jnp.where(column.astype(jnp.int32) == lanes(OBS), 1.0, 0.0).astype(BF16)


def through(v, parts_ref):
    rows = v.shape[0]
    both = stacked(v)
    high, low = dot(both, parts_ref[0], NT), dot(both, parts_ref[1], NT)
    return high[:rows] + (high[rows:] + low[:rows] + low[rows:])


def call(kernel, name, outs, operands, scratch=(), scalars=1, far=0, flops=10**8, moved=1 << 20, limit=16):
    vmem, smem = pl.BlockSpec(memory_space=pltpu.VMEM), pl.BlockSpec(memory_space=pltpu.SMEM)
    anywhere = pl.BlockSpec(memory_space=pltpu.MemorySpace.HBM)
    near_hbm = [
        pltpu.with_memory_space_constraint(value, pltpu.MemorySpace.HBM)
        for value in operands[scalars : scalars + far]
    ]
    return pl.pallas_call(
        kernel,
        out_shape=tuple(jax.ShapeDtypeStruct(*out) for out in outs),
        in_specs=[smem] * scalars + [anywhere] * far + [vmem] * (len(operands) - scalars - far),
        out_specs=(vmem,) * len(outs),
        scratch_shapes=list(scratch),
        cost_estimate=pl.CostEstimate(flops=flops, bytes_accessed=moved, transcendentals=0),
        compiler_params=pltpu.CompilerParams(vmem_limit_bytes=limit << 20),
        name=name,
    )(*operands[:scalars], *near_hbm, *operands[scalars + far :])


PARTS = ((2, N, N), BF16)
VECTOR = ((8, N), F32)


def keep_parts(values_ref, parts_ref):
    for r in range(0, N, 64):
        at = pl.ds(r, 64)
        parts_ref[0, at, :], parts_ref[1, at, :] = split2(values_ref[at, :])


def keep_columns(rows_ref, kept_ref, start):
    turned = jnp.transpose(rows_ref[...].astype(F32))
    for k in range(rows_ref.shape[0]):
        kept_ref[k, start : start + N, :] = jnp.broadcast_to(turned[:, k : k + 1], (N, LANES))


def clear_edges(padded_ref):
    edge = jnp.zeros((PIECES, REACH, LANES), F32)
    padded_ref[:, 0:REACH, :] = edge
    padded_ref[:, REACH + N : N + 2 * REACH, :] = edge


def start_identity(padded_ref):
    clear_edges(padded_ref)
    row = lax.broadcasted_iota(jnp.int32, (N, LANES), 0)
    for j in range(PIECES):
        padded_ref[j, REACH : REACH + N, :] = jnp.where(row == lanes(N, LANES) + LANES * j, 1.0, 0.0)


def keep_map(padded_ref, map_ref, parts_ref=None):
    for r in range(0, N, 64):
        for j in range(PIECES):
            at, cols = slice(r, r + 64), slice(LANES * j, LANES * (j + 1))
            value = padded_ref[j, REACH + r : REACH + r + 64, :]
            map_ref[at, cols] = value
            if parts_ref is not None:
                parts_ref[0, at, cols], parts_ref[1, at, cols] = split2(value)


def diffused(padded_ref, j, first, size, centre):
    at = lambda by: padded_ref[j, pl.ds(first + by, size), :]
    return centre * at(0) + (0.5 * DIFFUSION) * (at(1) + at(-1))


def filter_map(offsets, upwind, courant, obs_cells, gains, observed):
    steps = offsets.shape[0]

    def kernel(
        offs_ref, cells_ref, up_far, c_far, obs_far, y_far, gains_far,
        map_ref, held_ref, moved_ref, picked_ref, ups_ref, cs_ref,
        up_ref, c_ref, obs_ref, y_ref, gains_ref, sem
    ):
        pairs = ((up_far, up_ref), (c_far, c_ref), (obs_far, obs_ref), (y_far, y_ref))
        copies = [pltpu.make_async_copy(a, b, sem.at[i]) for i, (a, b) in enumerate(pairs)]
        for copy in copies:
            copy.start()
        fetch = lambda k: pltpu.make_async_copy(gains_far.at[k], gains_ref.at[k], sem.at[4 + k])
        for k in range(steps):
            fetch(k).start()
        start_identity(held_ref)
        for copy in copies:
            copy.wait()
        keep_columns(up_ref, ups_ref, 0)
        keep_columns(c_ref, cs_ref, 0)
        head = lax.broadcasted_iota(jnp.int32, (8, 1), 0) == 0

        def one(k, vec):
            step = Step(k, offs_ref, up_ref, c_ref)
            s = one_hot(obs_ref[pl.ds(k, 1), :])
            fetch(k).wait()
            gain = RELAXATION * s.astype(F32) + gains_ref[k]
            for r in range(0, N, CELLS):
                ups, cs = ups_ref[k, r : r + CELLS, :], cs_ref[k, r : r + CELLS, :]
                for j in range(PIECES):
                    at = lambda by: held_ref[j, pl.ds(REACH + r + by, CELLS), :]
                    arrived = at(step.offs[0])
                    for band in range(1, BANDS):
                        arrived = jnp.where(ups == band, at(step.offs[band]), arrived)
                    spread = diffused(held_ref, j, REACH + r, CELLS, 1.0 - cs - DIFFUSION)
                    moved_ref[j, r : r + CELLS, :] = spread + cs * arrived
            for o in range(OBS):
                for j in range(PIECES):
                    cols = slice(LANES * j, LANES * (j + 1))
                    picked_ref[o : o + 1, cols] = moved_ref[j, pl.ds(cells_ref[k, o], 1), :]
            seen_hi, seen_lo = split2(picked_ref[...])
            seen = jnp.concatenate([seen_hi, seen_lo] * 2, axis=0)
            turned = jnp.transpose(jnp.concatenate([gain, gain], axis=0))
            factors = jnp.concatenate(split2(turned), axis=1)
            for r in range(0, N, 256):
                at = slice(r, r + 256)
                corrected = pieces(dot(factors[at], seen))
                for j in range(PIECES):
                    held_ref[j, REACH + r : REACH + r + 256, :] = moved_ref[j, at, :] - corrected[j]

            high, low = split2(gain)
            kk = jnp.concatenate([high, high, low, low], axis=0)
            s2 = jnp.concatenate([s] * 2, axis=0)
            y2 = jnp.concatenate([y_ref[pl.ds(k, 1), :]] * 2, axis=1)
            p = step.apply(vec)
            return p - correction(observed_part(p, s2) - jnp.where(head, y2, 0.0), kk)

        vec = lax.fori_loop(0, steps, one, jnp.zeros((8, N), F32))
        map_ref[N:ROWS, :] = vec
        keep_map(held_ref, map_ref)

    return call(
        kernel,
        "filter_map",
        (((ROWS, N), F32),),
        (offsets, obs_cells, upwind, courant, obs_cells, observed, gains),
        scratch=[
            pltpu.VMEM((PIECES, N + 2 * REACH, LANES), F32),
            pltpu.VMEM((PIECES, N, LANES), F32),
            pltpu.VMEM((OBS, N), F32),
            pltpu.VMEM((steps, N, LANES), F32),
            pltpu.VMEM((steps, N, LANES), F32),
            pltpu.VMEM((steps, N), jnp.int32),
            pltpu.VMEM((steps, N), F32),
            pltpu.VMEM((steps, OBS), jnp.int32),
            pltpu.VMEM((steps, OBS), F32),
            pltpu.VMEM((steps, OBS, N), F32),
            pltpu.SemaphoreType.DMA((4 + steps,)),
        ],
        scalars=2,
        far=5,
        flops=16 * 10**9,
        moved=4 << 20,
        limit=28,
    )[0]


def smoother_map(offsets, upwind, courant, smooth_gain):
    steps = offsets.shape[0]

    def kernel(offs_ref, up_ref, c_ref, sg_ref, map_ref, parts_ref, held_ref, out_ref, ups_ref, cs_ref, gains_ref):
        outside = jnp.full((REACH, LANES), -1.0, F32)
        for k in range(steps):
            ups_ref[k, 0:REACH, :] = outside
            ups_ref[k, REACH + N : N + 2 * REACH, :] = outside
        keep_columns(up_ref, ups_ref, REACH)
        keep_columns(c_ref, cs_ref, 0)
        keep_columns(sg_ref, gains_ref, 0)
        start_identity(held_ref.at[0])
        clear_edges(held_ref.at[1])
        clear_edges(out_ref)

        def one(i, carry):
            k = steps - 1 - i
            offs = [offs_ref[k, band] for band in range(BANDS)]
            now, later = held_ref.at[lax.rem(i, 2)], held_ref.at[lax.rem(i + 1, 2)]
            for r in range(0, N, CELLS):
                cs = cs_ref[k, r : r + CELLS, :]
                for j in range(PIECES):
                    at = slice(REACH + r, REACH + r + CELLS)
                    out_ref[j, at, :] = cs * now[j, at, :]
            for r in range(0, N, CELLS):
                froms = [pl.ds(REACH + r - offs[band], CELLS) for band in range(BANDS)]
                taken = [ups_ref[k, froms[band], :] == band for band in range(BANDS)]
                centre = 1.0 - cs_ref[k, r : r + CELLS, :] - DIFFUSION
                gain = gains_ref[k, r : r + CELLS, :]
                for j in range(PIECES):
                    total = diffused(now, j, REACH + r, CELLS, centre)
                    for band in range(BANDS):
                        total = total + jnp.where(taken[band], out_ref[j, froms[band], :], 0.0)
                    later[j, REACH + r : REACH + r + CELLS, :] = gain * total
            return carry

        lax.fori_loop(0, steps, one, 0)
        keep_map(held_ref.at[steps % 2], map_ref, parts_ref)

    return call(
        kernel,
        "smoother_map",
        (((N, N), F32), PARTS),
        (offsets, upwind, courant, smooth_gain),
        scratch=[
            pltpu.VMEM((2, PIECES, N + 2 * REACH, LANES), F32),
            pltpu.VMEM((PIECES, N + 2 * REACH, LANES), F32),
            pltpu.VMEM((steps, N + 2 * REACH, LANES), F32),
            pltpu.VMEM((steps, N, LANES), F32),
            pltpu.VMEM((steps, N, LANES), F32),
        ],
        flops=8 * 10**9,
        moved=2 << 20,
        limit=28,
    )


def compose(flag, mine, other, keep=True, parts=False, other_parts=False, far=False):
    rows = mine.shape[0]
    affine = rows > N
    kinds = (("out", keep, ((rows, N), F32)), ("off", affine, VECTOR), ("parts", parts, PARTS), ("other", other_parts, PARTS))

    def kernel(flag_ref, mine_ref, other_ref, *more):
        names = [name for name, wanted, _ in kinds if wanted]
        refs = dict(zip(names, more[: len(names)], strict=True))
        if far:
            *held, sem = more[len(names) :]

            @pl.when(flag_ref[0] != 2)
            def _():
                pairs = enumerate(zip((mine_ref, other_ref), held, strict=True))
                copies = [pltpu.make_async_copy(a, b, sem.at[i]) for i, (a, b) in pairs]
                for copy in copies:
                    copy.start()
                for copy in copies:
                    copy.wait()

            mine_ref, other_ref = held

        def product(first_ref, second_ref):
            if other_parts:
                keep_parts(other_ref, refs["other"])
            high, low = split2(first_ref[0:N, :])
            for start in (0, 256):
                at = pl.ds(start, 256)
                both = stacked(second_ref[at, :])
                big = dot(both, high)
                total = big[:256] + (big[256:] + dot(both[:256], low))
                if keep:
                    refs["out"][at, :] = total
                if parts:
                    refs["parts"][0, at, :], refs["parts"][1, at, :] = split2(total)
            if affine:
                both = stacked(first_ref[N:ROWS, :])
                halves = split2(second_ref[0:N, :])
                big, small = dot(both, halves[0], NT), dot(both, halves[1], NT)
                offset = big[:8] + (big[8:] + small[:8] + small[8:]) + second_ref[N:ROWS, :]
                refs["off"][...] = offset
                if keep:
                    refs["out"][N:ROWS, :] = offset

        @pl.when(flag_ref[0] == 1)
        def _():
            product(other_ref, mine_ref)

        @pl.when(flag_ref[0] == 0)
        def _():
            product(mine_ref, other_ref)

    outs = tuple(shape for _, wanted, shape in kinds if wanted)
    scratch = [pltpu.VMEM((rows, N), F32)] * 2 + [pltpu.SemaphoreType.DMA((2,))]
    return call(
        kernel,
        "compose",
        outs,
        (flag, mine, other),
        scratch=scratch if far else (),
        far=2 if far else 0,
        flops=10**9,
        moved=5 << 20,
    )


def parted(maps):
    def kernel(map_ref, parts_ref, off_ref):
        keep_parts(map_ref, parts_ref)
        off_ref[...] = map_ref[N:ROWS, :]

    return call(kernel, "parted", (PARTS, VECTOR), (maps,), scalars=0, flops=10**8, moved=2 << 20)


def hop(place, mark, state, got, parts, offset):
    def kernel(place_ref, state_ref, got_ref, parts_ref, off_ref, new_ref, sent_ref):
        new = jnp.where(place_ref[0] == mark, got_ref[...], state_ref[...])
        new_ref[...] = new
        sent_ref[...] = through(new, parts_ref) + off_ref[...]

    return call(kernel, "hop", (VECTOR, VECTOR), (place, state, got, parts, offset))


def descend(place, mark, state, got, quad, quad_off, pair, pair_off, own, own_off):
    def kernel(place_ref, state_ref, got_ref, quad_ref, qo_ref, pair_ref, po_ref, own_ref, oo_ref, new_ref, sent_ref):
        new_ref[...] = jnp.where(place_ref[0] == mark, got_ref[...], state_ref[...])

        @pl.when(place_ref[1] == 1)
        def _():
            new_ref[...] = through(new_ref[...], quad_ref) + qo_ref[...]

        @pl.when(place_ref[2] == 1)
        def _():
            new_ref[...] = through(new_ref[...], pair_ref) + po_ref[...]

        sent_ref[...] = through(new_ref[...], own_ref) + oo_ref[...]

    operands = (place, state, got, quad, quad_off, pair, pair_off, own, own_off)
    return call(kernel, "descend", (VECTOR, VECTOR), operands)


def joined(flag, mine, other, my_parts, other_parts):
    def kernel(flag_ref, mine_ref, other_ref, mp_ref, op_ref, out_ref):
        @pl.when(flag_ref[0] == 1)
        def _():
            out_ref[...] = through(other_ref[...], mp_ref) + mine_ref[...]

        @pl.when(flag_ref[0] == 0)
        def _():
            out_ref[...] = through(mine_ref[...], op_ref) + other_ref[...]

    return call(kernel, "joined", (VECTOR,), (flag, mine, other, my_parts, other_parts))[0]


def smoothing(steps, diff, offs_ref, up_ref, c_ref, sg_ref, u_ref, store=None):
    def one(i, diff):
        k = steps - 1 - i
        step = Step(k, offs_ref, up_ref, c_ref)
        if store is not None:
            store(k, diff)
        at = pl.ds(k, 1)
        return sg_ref[at, :] * step.apply_transposed(diff + u_ref[at, :])

    return lax.fori_loop(0, steps, one, diff)


def one_hots(obs_cells):
    steps = obs_cells.shape[0]

    def kernel(obs_ref, hots_ref):
        for k in range(steps):
            hots_ref[k] = one_hot(obs_ref[k : k + 1, :])

    return call(kernel, "one_hots", (((steps, OBS, N), BF16),), (obs_cells,), scalars=0)[0]


def forward(place, offsets, upwind, courant, smooth_gain, hots, gains, observed, state, got):
    steps = offsets.shape[0]

    def kernel(
        place_ref, offs_ref, s_far, gains_far, up_ref, c_ref, sg_ref, y_ref, state_ref, got_ref,
        filt_ref, upd_ref, end_ref, s_ref, gains_ref, sem
    ):
        def fetch(k):
            return (
                pltpu.make_async_copy(s_far.at[k], s_ref.at[k], sem.at[k]),
                pltpu.make_async_copy(gains_far.at[k], gains_ref.at[k], sem.at[steps + k]),
            )

        for k in range(steps):
            for copy in fetch(k):
                copy.start()
        first = lax.broadcasted_iota(jnp.int32, (8, 1), 0) == 0

        def one(k, vec):
            step = Step(k, offs_ref, up_ref, c_ref)
            for copy in fetch(k):
                copy.wait()
            s = s_ref[k]
            kk = gain_rows(s, gains_ref[k])
            s2 = jnp.concatenate([s] * 2, axis=0)
            y2 = jnp.concatenate([y_ref[pl.ds(k, 1), :]] * 2, axis=1)
            p = step.apply(vec)
            update = -correction(observed_part(p, s2) - jnp.where(first, y2, 0.0), kk)
            vec = p + update
            filt_ref[pl.ds(k, 1), :] = vec[0:1]
            upd_ref[pl.ds(k, 1), :] = update[0:1]
            return vec

        start = jnp.where(place_ref[0] == 1, got_ref[...], state_ref[...])
        lax.fori_loop(0, steps, one, start)
        zeros = jnp.zeros((8, N), F32)
        end_ref[...] = smoothing(steps, zeros, offs_ref, up_ref, c_ref, sg_ref, upd_ref)

    return call(
        kernel,
        "forward",
        (((steps, N), F32), ((steps, N), F32), VECTOR),
        (place, offsets, hots, gains, upwind, courant, smooth_gain, observed, state, got),
        scratch=[
            pltpu.VMEM((steps, OBS, N), BF16),
            pltpu.VMEM((steps, OBS, N), F32),
            pltpu.SemaphoreType.DMA((2 * steps,)),
        ],
        scalars=2,
        far=2,
        flops=4 * 10**9,
        moved=3 << 20,
    )


def smooth(place, offsets, upwind, courant, smooth_gain, updates, filtered, top, got):
    steps = offsets.shape[0]

    def kernel(place_ref, offs_ref, up_ref, c_ref, sg_ref, u_ref, x_ref, top_ref, got_ref, out_ref):
        def store(k, diff):
            at = pl.ds(k, 1)
            out_ref[at, :] = x_ref[at, :] + diff[0:1]

        diff = jnp.where(place_ref[0] == 0, got_ref[...], top_ref[...])
        smoothing(steps, diff, offs_ref, up_ref, c_ref, sg_ref, u_ref, store)

    return call(
        kernel,
        "smooth",
        (((steps, N), F32),),
        (place, offsets, upwind, courant, smooth_gain, updates, filtered, top, got),
        scalars=2,
    )[0]


def on_device(initial, offsets, upwind, courant, obs_cells, gains, observed, smooth_gain):
    place = lax.axis_index("tm")
    x, y, core = place // 8, (place // 2) % 4, place % 2

    def moved(values, to, senders):
        return lax.ppermute(values, "tm", [(i, to(i)) for i in range(32) if senders(i)])

    even = lambda i: i % 2 == 0
    odd = lambda i: i % 2 == 1
    ints = lambda *values: jnp.stack([jnp.asarray(v, jnp.int32) for v in values])
    never = jnp.zeros((1,), jnp.int32)
    at_core = ints(core)
    on_even = lambda flag: ints(jnp.where(core == 0, flag, 2))
    on_odd = lambda flag: ints(jnp.where(core == 1, flag, 2))
    y_even, y_low = ints(y % 2 == 0), ints(y < 2)
    start_row = jnp.broadcast_to(initial[None, :], (8, N))
    zeros = jnp.zeros((8, N), F32)

    after = lambda value, *before: lax.optimization_barrier((value, *before))[0]

    fmap = filter_map(offsets, upwind, courant, obs_cells, gains, observed)
    fmap_odd = moved(fmap, lambda i: i - 1, odd)
    fpair, fpair_o = compose(on_even(0), fmap, fmap_odd)
    fpair_other = moved(fpair, lambda i: i ^ 2, even)
    smap, smap_p = smoother_map(offsets, after(upwind, fpair_o), courant, smooth_gain)
    fquad, fquad_o = compose(on_even(y % 2), fpair, fpair_other)
    fquad_other = moved(fquad, lambda i: i ^ 6, even)
    smap_even = moved(after(smap, fquad_o), lambda i: i + 1, even)
    spair, spair_p, smap_ep = compose(
        on_odd(0), smap, smap_even, parts=True, other_parts=True, far=True
    )
    fpair_op, fpair_oo = parted(fpair_other)
    fmap_p, fmap_o = parted(fmap)
    hots = one_hots(after(obs_cells, fquad_o))
    foct_o, foct_p = compose(after(on_even(y // 2), hots), fquad, fquad_other, keep=False, parts=True)

    place3 = ints(x, y >= 2, y % 2 == 1)
    ahead_of = lambda v: moved(v, lambda i: i + 8, lambda i: even(i) and i < 24)
    state, sent = hop(place3, 0, start_row, start_row, foct_p, foct_o)
    got = ahead_of(sent)
    spair_other = moved(after(spair, sent), lambda i: i ^ 2, odd)
    fquad_op, fquad_oo = parted(fquad_other)
    state, sent = hop(place3, 1, after(state, fquad_oo), got, foct_p, foct_o)
    got = ahead_of(sent)
    state, sent = hop(place3, 2, state, got, foct_p, foct_o)
    got = ahead_of(sent)
    squad, squad_p, spair_op = compose(
        on_odd(1 - y % 2), spair, after(spair_other, sent), parts=True, other_parts=True, far=True
    )
    squad_other = moved(squad, lambda i: i ^ 6, odd)
    state, sent = descend(
        place3, 3, after(state, squad_p), got, fquad_op, fquad_oo, fpair_op, fpair_oo, fmap_p, fmap_o
    )
    got = moved(sent, lambda i: i + 1, even)
    filtered, updates, own = forward(
        at_core, offsets, upwind, courant, smooth_gain, hots, gains, observed, state, got
    )
    soct_p, squad_op = compose(
        on_odd(1 - y // 2),
        squad,
        after(squad_other, own),
        keep=False,
        parts=True,
        other_parts=True,
        far=True,
    )

    pair = joined(never, own, moved(own, lambda i: i + 1, even), smap_p, smap_ep)
    pair_other = moved(pair, lambda i: i ^ 2, odd)
    quad = joined(y_even, pair, pair_other, spair_p, spair_op)
    quad_other = moved(quad, lambda i: i ^ 6, odd)
    octet = joined(y_low, quad, quad_other, squad_p, squad_op)
    place3 = ints(x, y < 2, y % 2 == 0)
    behind = lambda v: moved(v, lambda i: i - 8, lambda i: odd(i) and i >= 8)
    got = behind(octet)
    top, sent = hop(place3, 2, zeros, got, soct_p, octet)
    got = behind(sent)
    top, sent = hop(place3, 1, top, got, soct_p, octet)
    got = behind(sent)
    top, sent = descend(place3, 0, top, got, squad_op, quad_other, spair_op, pair_other, smap_p, own)
    got = moved(sent, lambda i: i - 1, odd)
    smoothed = smooth(
        at_core, offsets, upwind, courant, smooth_gain, updates, filtered, top, got
    )
    return filtered, smoothed


def solution(mesh):
    row = P("tm", None)
    in_specs = (P(), row, row, row, row, P("tm", None, None), row, row)
    return jax.shard_map(on_device, mesh=mesh, in_specs=in_specs, out_specs=(row, row), check_vma=False)
```

```python
import jax
import jax.numpy as jnp
from jax import lax
from jax.experimental import pallas as pl
from jax.experimental.pallas import tpu as pltpu
from jax.sharding import PartitionSpec as P


N = 512
OBS = 64
BANDS = 4
REACH = 32
DIFFUSION = 0.25
RELAXATION = 0.02
ROWS = N + 8
LANES = 128
PIECES = N // LANES
CELLS = 32
F32 = jnp.float32
BF16 = jnp.bfloat16
NT = (((1,), (1,)), ((), ()))
NN = (((1,), (0,)), ((), ()))


def lanes(rows, count=N):
    return lax.broadcasted_iota(jnp.int32, (rows, count), 1)


def pieces(v):
    return [v[:, LANES * j : LANES * (j + 1)] for j in range(PIECES)]


def ahead(parts, by):
    turn = jnp.where(by == 0, 0, LANES - by)
    turned = [pltpu.roll(part, turn, 1) for part in parts]
    here = lanes(1, LANES) + by < LANES
    return [jnp.where(here, turned[j], turned[(j + 1) % PIECES]) for j in range(PIECES)]


def neighbours(v):
    lane = lanes(1)
    left = jnp.where(lane > 0, 0.5 * DIFFUSION, 0.0)
    right = jnp.where(lane < N - 1, 0.5 * DIFFUSION, 0.0)
    return right * pltpu.roll(v, N - 1, 1) + left * pltpu.roll(v, 1, 1)


class Step:
    def __init__(self, k, offs_ref, up_ref, c_ref):
        self.offs = [offs_ref[k, band] for band in range(BANDS)]
        self.up = up_ref[pl.ds(k, 1), :]
        courant = c_ref[pl.ds(k, 1), :]
        reach = jnp.full_like(self.up, self.offs[0])
        for band in range(1, BANDS):
            reach = jnp.where(self.up == band, self.offs[band], reach)
        at = lanes(1) + reach
        inside = (at >= 0) & (at < N)
        self.centre = 1.0 - courant - DIFFUSION
        self.advected = jnp.where(inside, courant, 0.0)

    def apply(self, v):
        base = pieces(pltpu.roll(v, REACH, 1))
        ups = pieces(self.up)
        moved = ahead(base, self.offs[0] + REACH)
        for band in range(1, BANDS):
            other = ahead(base, self.offs[band] + REACH)
            moved = [jnp.where(ups[j] == band, other[j], moved[j]) for j in range(PIECES)]
        return self.centre * v + neighbours(v) + self.advected * jnp.concatenate(moved, axis=1)

    def apply_transposed(self, v):
        out = pieces(pltpu.roll(self.advected * v, REACH, 1))
        ups = pieces(pltpu.roll(self.up, REACH, 1))
        total = pieces(self.centre * v + neighbours(v))
        for band in range(BANDS):
            own = [jnp.where(ups[j] == band, out[j], 0.0) for j in range(PIECES)]
            shifted = ahead(own, REACH - self.offs[band])
            total = [total[j] + shifted[j] for j in range(PIECES)]
        return jnp.concatenate(total, axis=1)


def dot(a, b, dims=NN):
    return lax.dot_general(a, b, dims, preferred_element_type=F32)


def split2(v):
    hi = v.astype(BF16)
    return hi, (v - hi.astype(F32)).astype(BF16)


def stacked(v):
    hi = v.astype(BF16).astype(F32)
    return jnp.concatenate([hi, v - hi], axis=0).astype(BF16)


def observed_part(p, s2):
    rows = p.shape[0]
    both = dot(stacked(p), s2, NT)
    return both[:rows] + both[rows:]


def gain_rows(s, gains):
    hi, lo = split2(RELAXATION * s.astype(F32) + gains)
    return jnp.concatenate([hi, hi, lo, lo], axis=0)


def correction(e2, kk):
    hi = e2.astype(BF16).astype(F32)
    mixed = jnp.where(lanes(1, 2 * OBS) >= OBS, e2 - hi, hi)
    return dot(jnp.concatenate([mixed, mixed], axis=1).astype(BF16), kk)


def one_hot(obs_row):
    own = lax.broadcasted_iota(jnp.int32, (OBS, OBS), 0) == lanes(OBS, OBS)
    column = jnp.sum(jnp.where(own, obs_row.astype(F32), 0.0), axis=1, keepdims=True)
    return jnp.where(column.astype(jnp.int32) == lanes(OBS), 1.0, 0.0).astype(BF16)


def through(v, parts_ref):
    rows = v.shape[0]
    both = stacked(v)
    high, low = dot(both, parts_ref[0], NT), dot(both, parts_ref[1], NT)
    return high[:rows] + (high[rows:] + low[:rows] + low[rows:])


def call(kernel, outs, operands, scratch=(), scalars=1, far=0, flops=10**8, moved=1 << 20, limit=16):
    vmem, smem = pl.BlockSpec(memory_space=pltpu.VMEM), pl.BlockSpec(memory_space=pltpu.SMEM)
    anywhere = pl.BlockSpec(memory_space=pltpu.MemorySpace.HBM)
    near_hbm = [
        pltpu.with_memory_space_constraint(value, pltpu.MemorySpace.HBM)
        for value in operands[scalars : scalars + far]
    ]
    return pl.pallas_call(
        kernel,
        out_shape=tuple(jax.ShapeDtypeStruct(*out) for out in outs),
        in_specs=[smem] * scalars + [anywhere] * far + [vmem] * (len(operands) - scalars - far),
        out_specs=(vmem,) * len(outs),
        scratch_shapes=list(scratch),
        cost_estimate=pl.CostEstimate(flops=flops, bytes_accessed=moved, transcendentals=0),
        compiler_params=pltpu.CompilerParams(vmem_limit_bytes=limit << 20),
    )(*operands[:scalars], *near_hbm, *operands[scalars + far :])


PARTS = ((2, N, N), BF16)
VECTOR = ((8, N), F32)


def keep_parts(values_ref, parts_ref):
    for r in range(0, N, 64):
        at = pl.ds(r, 64)
        parts_ref[0, at, :], parts_ref[1, at, :] = split2(values_ref[at, :])


def keep_columns(rows_ref, kept_ref, start):
    turned = jnp.transpose(rows_ref[...].astype(F32))
    for k in range(rows_ref.shape[0]):
        kept_ref[k, start : start + N, :] = jnp.broadcast_to(turned[:, k : k + 1], (N, LANES))


def clear_edges(padded_ref):
    edge = jnp.zeros((PIECES, REACH, LANES), F32)
    padded_ref[:, 0:REACH, :] = edge
    padded_ref[:, REACH + N : N + 2 * REACH, :] = edge


def start_identity(padded_ref):
    clear_edges(padded_ref)
    row = lax.broadcasted_iota(jnp.int32, (N, LANES), 0)
    for j in range(PIECES):
        padded_ref[j, REACH : REACH + N, :] = jnp.where(row == lanes(N, LANES) + LANES * j, 1.0, 0.0)


def keep_map(padded_ref, map_ref, parts_ref=None):
    for r in range(0, N, 64):
        for j in range(PIECES):
            at, cols = slice(r, r + 64), slice(LANES * j, LANES * (j + 1))
            value = padded_ref[j, REACH + r : REACH + r + 64, :]
            map_ref[at, cols] = value
            if parts_ref is not None:
                parts_ref[0, at, cols], parts_ref[1, at, cols] = split2(value)


def diffused(padded_ref, j, first, size, centre):
    at = lambda by: padded_ref[j, pl.ds(first + by, size), :]
    return centre * at(0) + (0.5 * DIFFUSION) * (at(1) + at(-1))


def filter_map(offsets, upwind, courant, obs_cells, gains, observed):
    steps = offsets.shape[0]

    def kernel(
        offs_ref, cells_ref, up_far, c_far, obs_far, y_far, gains_far,
        map_ref, held_ref, moved_ref, picked_ref, ups_ref, cs_ref,
        up_ref, c_ref, obs_ref, y_ref, gains_ref, sem
    ):
        pairs = ((up_far, up_ref), (c_far, c_ref), (obs_far, obs_ref), (y_far, y_ref))
        copies = [pltpu.make_async_copy(a, b, sem.at[i]) for i, (a, b) in enumerate(pairs)]
        for copy in copies:
            copy.start()
        fetch = lambda k: pltpu.make_async_copy(gains_far.at[k], gains_ref.at[k], sem.at[4 + k])
        for k in range(steps):
            fetch(k).start()
        start_identity(held_ref)
        for copy in copies:
            copy.wait()
        keep_columns(up_ref, ups_ref, 0)
        keep_columns(c_ref, cs_ref, 0)
        head = lax.broadcasted_iota(jnp.int32, (8, 1), 0) == 0

        def one(k, vec):
            step = Step(k, offs_ref, up_ref, c_ref)
            s = one_hot(obs_ref[pl.ds(k, 1), :])
            fetch(k).wait()
            gain = RELAXATION * s.astype(F32) + gains_ref[k]
            for r in range(0, N, CELLS):
                ups, cs = ups_ref[k, r : r + CELLS, :], cs_ref[k, r : r + CELLS, :]
                for j in range(PIECES):
                    at = lambda by: held_ref[j, pl.ds(REACH + r + by, CELLS), :]
                    arrived = at(step.offs[0])
                    for band in range(1, BANDS):
                        arrived = jnp.where(ups == band, at(step.offs[band]), arrived)
                    spread = diffused(held_ref, j, REACH + r, CELLS, 1.0 - cs - DIFFUSION)
                    moved_ref[j, r : r + CELLS, :] = spread + cs * arrived
            for o in range(OBS):
                for j in range(PIECES):
                    cols = slice(LANES * j, LANES * (j + 1))
                    picked_ref[o : o + 1, cols] = moved_ref[j, pl.ds(cells_ref[k, o], 1), :]
            seen_hi, seen_lo = split2(picked_ref[...])
            seen = jnp.concatenate([seen_hi, seen_lo] * 2, axis=0)
            turned = jnp.transpose(jnp.concatenate([gain, gain], axis=0))
            factors = jnp.concatenate(split2(turned), axis=1)
            for r in range(0, N, 256):
                at = slice(r, r + 256)
                corrected = pieces(dot(factors[at], seen))
                for j in range(PIECES):
                    held_ref[j, REACH + r : REACH + r + 256, :] = moved_ref[j, at, :] - corrected[j]

            high, low = split2(gain)
            kk = jnp.concatenate([high, high, low, low], axis=0)
            s2 = jnp.concatenate([s] * 2, axis=0)
            y2 = jnp.concatenate([y_ref[pl.ds(k, 1), :]] * 2, axis=1)
            p = step.apply(vec)
            return p - correction(observed_part(p, s2) - jnp.where(head, y2, 0.0), kk)

        vec = lax.fori_loop(0, steps, one, jnp.zeros((8, N), F32))
        map_ref[N:ROWS, :] = vec
        keep_map(held_ref, map_ref)

    return call(
        kernel,
        (((ROWS, N), F32),),
        (offsets, obs_cells, upwind, courant, obs_cells, observed, gains),
        scratch=[
            pltpu.VMEM((PIECES, N + 2 * REACH, LANES), F32),
            pltpu.VMEM((PIECES, N, LANES), F32),
            pltpu.VMEM((OBS, N), F32),
            pltpu.VMEM((steps, N, LANES), F32),
            pltpu.VMEM((steps, N, LANES), F32),
            pltpu.VMEM((steps, N), jnp.int32),
            pltpu.VMEM((steps, N), F32),
            pltpu.VMEM((steps, OBS), jnp.int32),
            pltpu.VMEM((steps, OBS), F32),
            pltpu.VMEM((steps, OBS, N), F32),
            pltpu.SemaphoreType.DMA((4 + steps,)),
        ],
        scalars=2,
        far=5,
        flops=16 * 10**9,
        moved=4 << 20,
        limit=28,
    )[0]


def smoother_map(offsets, upwind, courant, smooth_gain):
    steps = offsets.shape[0]

    def kernel(offs_ref, up_ref, c_ref, sg_ref, map_ref, parts_ref, held_ref, out_ref, ups_ref, cs_ref, gains_ref):
        outside = jnp.full((REACH, LANES), -1.0, F32)
        for k in range(steps):
            ups_ref[k, 0:REACH, :] = outside
            ups_ref[k, REACH + N : N + 2 * REACH, :] = outside
        keep_columns(up_ref, ups_ref, REACH)
        keep_columns(c_ref, cs_ref, 0)
        keep_columns(sg_ref, gains_ref, 0)
        start_identity(held_ref.at[0])
        clear_edges(held_ref.at[1])
        clear_edges(out_ref)

        def one(i, carry):
            k = steps - 1 - i
            offs = [offs_ref[k, band] for band in range(BANDS)]
            now, later = held_ref.at[lax.rem(i, 2)], held_ref.at[lax.rem(i + 1, 2)]
            for r in range(0, N, CELLS):
                cs = cs_ref[k, r : r + CELLS, :]
                for j in range(PIECES):
                    at = slice(REACH + r, REACH + r + CELLS)
                    out_ref[j, at, :] = cs * now[j, at, :]
            for r in range(0, N, CELLS):
                froms = [pl.ds(REACH + r - offs[band], CELLS) for band in range(BANDS)]
                taken = [ups_ref[k, froms[band], :] == band for band in range(BANDS)]
                centre = 1.0 - cs_ref[k, r : r + CELLS, :] - DIFFUSION
                gain = gains_ref[k, r : r + CELLS, :]
                for j in range(PIECES):
                    total = diffused(now, j, REACH + r, CELLS, centre)
                    for band in range(BANDS):
                        total = total + jnp.where(taken[band], out_ref[j, froms[band], :], 0.0)
                    later[j, REACH + r : REACH + r + CELLS, :] = gain * total
            return carry

        lax.fori_loop(0, steps, one, 0)
        keep_map(held_ref.at[steps % 2], map_ref, parts_ref)

    return call(
        kernel,
        (((N, N), F32), PARTS),
        (offsets, upwind, courant, smooth_gain),
        scratch=[
            pltpu.VMEM((2, PIECES, N + 2 * REACH, LANES), F32),
            pltpu.VMEM((PIECES, N + 2 * REACH, LANES), F32),
            pltpu.VMEM((steps, N + 2 * REACH, LANES), F32),
            pltpu.VMEM((steps, N, LANES), F32),
            pltpu.VMEM((steps, N, LANES), F32),
        ],
        flops=8 * 10**9,
        moved=2 << 20,
        limit=28,
    )


def compose(flag, mine, other, keep=True, parts=False, other_parts=False, far=False):
    rows = mine.shape[0]
    affine = rows > N
    kinds = (("out", keep, ((rows, N), F32)), ("off", affine, VECTOR), ("parts", parts, PARTS), ("other", other_parts, PARTS))

    def kernel(flag_ref, mine_ref, other_ref, *more):
        names = [name for name, wanted, _ in kinds if wanted]
        refs = dict(zip(names, more[: len(names)], strict=True))
        if far:
            *held, sem = more[len(names) :]

            @pl.when(flag_ref[0] != 2)
            def _():
                pairs = enumerate(zip((mine_ref, other_ref), held, strict=True))
                copies = [pltpu.make_async_copy(a, b, sem.at[i]) for i, (a, b) in pairs]
                for copy in copies:
                    copy.start()
                for copy in copies:
                    copy.wait()

            mine_ref, other_ref = held

        def product(first_ref, second_ref):
            if other_parts:
                keep_parts(other_ref, refs["other"])
            high, low = split2(first_ref[0:N, :])
            for start in (0, 256):
                at = pl.ds(start, 256)
                both = stacked(second_ref[at, :])
                big = dot(both, high)
                total = big[:256] + (big[256:] + dot(both[:256], low))
                if keep:
                    refs["out"][at, :] = total
                if parts:
                    refs["parts"][0, at, :], refs["parts"][1, at, :] = split2(total)
            if affine:
                both = stacked(first_ref[N:ROWS, :])
                halves = split2(second_ref[0:N, :])
                big, small = dot(both, halves[0], NT), dot(both, halves[1], NT)
                offset = big[:8] + (big[8:] + small[:8] + small[8:]) + second_ref[N:ROWS, :]
                refs["off"][...] = offset
                if keep:
                    refs["out"][N:ROWS, :] = offset

        @pl.when(flag_ref[0] == 1)
        def _():
            product(other_ref, mine_ref)

        @pl.when(flag_ref[0] == 0)
        def _():
            product(mine_ref, other_ref)

    outs = tuple(shape for _, wanted, shape in kinds if wanted)
    scratch = [pltpu.VMEM((rows, N), F32)] * 2 + [pltpu.SemaphoreType.DMA((2,))]
    return call(
        kernel,
        outs,
        (flag, mine, other),
        scratch=scratch if far else (),
        far=2 if far else 0,
        flops=10**9,
        moved=5 << 20,
    )


def parted(maps):
    def kernel(map_ref, parts_ref, off_ref):
        keep_parts(map_ref, parts_ref)
        off_ref[...] = map_ref[N:ROWS, :]

    return call(kernel, (PARTS, VECTOR), (maps,), scalars=0, flops=10**8, moved=2 << 20)


def hop(place, mark, state, got, parts, offset):
    def kernel(place_ref, state_ref, got_ref, parts_ref, off_ref, new_ref, sent_ref):
        new = jnp.where(place_ref[0] == mark, got_ref[...], state_ref[...])
        new_ref[...] = new
        sent_ref[...] = through(new, parts_ref) + off_ref[...]

    return call(kernel, (VECTOR, VECTOR), (place, state, got, parts, offset))


def descend(place, mark, state, got, quad, quad_off, pair, pair_off, own, own_off):
    def kernel(place_ref, state_ref, got_ref, quad_ref, qo_ref, pair_ref, po_ref, own_ref, oo_ref, new_ref, sent_ref):
        new_ref[...] = jnp.where(place_ref[0] == mark, got_ref[...], state_ref[...])

        @pl.when(place_ref[1] == 1)
        def _():
            new_ref[...] = through(new_ref[...], quad_ref) + qo_ref[...]

        @pl.when(place_ref[2] == 1)
        def _():
            new_ref[...] = through(new_ref[...], pair_ref) + po_ref[...]

        sent_ref[...] = through(new_ref[...], own_ref) + oo_ref[...]

    operands = (place, state, got, quad, quad_off, pair, pair_off, own, own_off)
    return call(kernel, (VECTOR, VECTOR), operands)


def joined(flag, mine, other, my_parts, other_parts):
    def kernel(flag_ref, mine_ref, other_ref, mp_ref, op_ref, out_ref):
        @pl.when(flag_ref[0] == 1)
        def _():
            out_ref[...] = through(other_ref[...], mp_ref) + mine_ref[...]

        @pl.when(flag_ref[0] == 0)
        def _():
            out_ref[...] = through(mine_ref[...], op_ref) + other_ref[...]

    return call(kernel, (VECTOR,), (flag, mine, other, my_parts, other_parts))[0]


def smoothing(steps, diff, offs_ref, up_ref, c_ref, sg_ref, u_ref, store=None):
    def one(i, diff):
        k = steps - 1 - i
        step = Step(k, offs_ref, up_ref, c_ref)
        if store is not None:
            store(k, diff)
        at = pl.ds(k, 1)
        return sg_ref[at, :] * step.apply_transposed(diff + u_ref[at, :])

    return lax.fori_loop(0, steps, one, diff)


def one_hots(obs_cells):
    steps = obs_cells.shape[0]

    def kernel(obs_ref, hots_ref):
        for k in range(steps):
            hots_ref[k] = one_hot(obs_ref[k : k + 1, :])

    return call(kernel, (((steps, OBS, N), BF16),), (obs_cells,), scalars=0)[0]


def forward(place, offsets, upwind, courant, smooth_gain, hots, gains, observed, state, got):
    steps = offsets.shape[0]

    def kernel(
        place_ref, offs_ref, s_far, gains_far, up_ref, c_ref, sg_ref, y_ref, state_ref, got_ref,
        filt_ref, upd_ref, end_ref, s_ref, gains_ref, sem
    ):
        def fetch(k):
            return (
                pltpu.make_async_copy(s_far.at[k], s_ref.at[k], sem.at[k]),
                pltpu.make_async_copy(gains_far.at[k], gains_ref.at[k], sem.at[steps + k]),
            )

        for k in range(steps):
            for copy in fetch(k):
                copy.start()
        first = lax.broadcasted_iota(jnp.int32, (8, 1), 0) == 0

        def one(k, vec):
            step = Step(k, offs_ref, up_ref, c_ref)
            for copy in fetch(k):
                copy.wait()
            s = s_ref[k]
            kk = gain_rows(s, gains_ref[k])
            s2 = jnp.concatenate([s] * 2, axis=0)
            y2 = jnp.concatenate([y_ref[pl.ds(k, 1), :]] * 2, axis=1)
            p = step.apply(vec)
            update = -correction(observed_part(p, s2) - jnp.where(first, y2, 0.0), kk)
            vec = p + update
            filt_ref[pl.ds(k, 1), :] = vec[0:1]
            upd_ref[pl.ds(k, 1), :] = update[0:1]
            return vec

        start = jnp.where(place_ref[0] == 1, got_ref[...], state_ref[...])
        lax.fori_loop(0, steps, one, start)
        zeros = jnp.zeros((8, N), F32)
        end_ref[...] = smoothing(steps, zeros, offs_ref, up_ref, c_ref, sg_ref, upd_ref)

    return call(
        kernel,
        (((steps, N), F32), ((steps, N), F32), VECTOR),
        (place, offsets, hots, gains, upwind, courant, smooth_gain, observed, state, got),
        scratch=[
            pltpu.VMEM((steps, OBS, N), BF16),
            pltpu.VMEM((steps, OBS, N), F32),
            pltpu.SemaphoreType.DMA((2 * steps,)),
        ],
        scalars=2,
        far=2,
        flops=4 * 10**9,
        moved=3 << 20,
    )


def smooth(place, offsets, upwind, courant, smooth_gain, updates, filtered, top, got):
    steps = offsets.shape[0]

    def kernel(place_ref, offs_ref, up_ref, c_ref, sg_ref, u_ref, x_ref, top_ref, got_ref, out_ref):
        def store(k, diff):
            at = pl.ds(k, 1)
            out_ref[at, :] = x_ref[at, :] + diff[0:1]

        diff = jnp.where(place_ref[0] == 0, got_ref[...], top_ref[...])
        smoothing(steps, diff, offs_ref, up_ref, c_ref, sg_ref, u_ref, store)

    return call(
        kernel,
        (((steps, N), F32),),
        (place, offsets, upwind, courant, smooth_gain, updates, filtered, top, got),
        scalars=2,
    )[0]


def on_device(initial, offsets, upwind, courant, obs_cells, gains, observed, smooth_gain):
    place = lax.axis_index("tm")
    x, y, core = place // 8, (place // 2) % 4, place % 2

    def moved(values, to, senders):
        return lax.ppermute(values, "tm", [(i, to(i)) for i in range(32) if senders(i)])

    even = lambda i: i % 2 == 0
    odd = lambda i: i % 2 == 1
    ints = lambda *values: jnp.stack([jnp.asarray(v, jnp.int32) for v in values])
    never = jnp.zeros((1,), jnp.int32)
    at_core = ints(core)
    on_even = lambda flag: ints(jnp.where(core == 0, flag, 2))
    on_odd = lambda flag: ints(jnp.where(core == 1, flag, 2))
    y_even, y_low = ints(y % 2 == 0), ints(y < 2)
    start_row = jnp.broadcast_to(initial[None, :], (8, N))
    zeros = jnp.zeros((8, N), F32)

    after = lambda value, *before: lax.optimization_barrier((value, *before))[0]

    fmap = filter_map(offsets, upwind, courant, obs_cells, gains, observed)
    fmap_odd = moved(fmap, lambda i: i - 1, odd)
    fpair, fpair_o = compose(on_even(0), fmap, fmap_odd)
    fpair_other = moved(fpair, lambda i: i ^ 2, even)
    smap, smap_p = smoother_map(offsets, after(upwind, fpair_o), courant, smooth_gain)
    fquad, fquad_o = compose(on_even(y % 2), fpair, fpair_other)
    fquad_other = moved(fquad, lambda i: i ^ 6, even)
    smap_even = moved(after(smap, fquad_o), lambda i: i + 1, even)
    spair, spair_p, smap_ep = compose(
        on_odd(0), smap, smap_even, parts=True, other_parts=True, far=True
    )
    fpair_op, fpair_oo = parted(fpair_other)
    fmap_p, fmap_o = parted(fmap)
    hots = one_hots(after(obs_cells, fquad_o))
    foct_o, foct_p = compose(after(on_even(y // 2), hots), fquad, fquad_other, keep=False, parts=True)

    place3 = ints(x, y >= 2, y % 2 == 1)
    ahead_of = lambda v: moved(v, lambda i: i + 8, lambda i: even(i) and i < 24)
    state, sent = hop(place3, 0, start_row, start_row, foct_p, foct_o)
    got = ahead_of(sent)
    spair_other = moved(after(spair, sent), lambda i: i ^ 2, odd)
    fquad_op, fquad_oo = parted(fquad_other)
    state, sent = hop(place3, 1, after(state, fquad_oo), got, foct_p, foct_o)
    got = ahead_of(sent)
    state, sent = hop(place3, 2, after(state, fpair_oo, fmap_o), got, foct_p, foct_o)
    got = ahead_of(sent)
    squad, squad_p, spair_op = compose(
        on_odd(1 - y % 2), spair, after(spair_other, sent), parts=True, other_parts=True, far=True
    )
    squad_other = moved(squad, lambda i: i ^ 6, odd)
    state, sent = descend(
        place3, 3, after(state, squad_p), got, fquad_op, fquad_oo, fpair_op, fpair_oo, fmap_p, fmap_o
    )
    got = moved(sent, lambda i: i + 1, even)
    filtered, updates, own = forward(
        at_core, offsets, upwind, courant, smooth_gain, hots, gains, observed, state, got
    )
    soct_p, squad_op = compose(
        on_odd(1 - y // 2),
        squad,
        after(squad_other, own),
        keep=False,
        parts=True,
        other_parts=True,
        far=True,
    )

    pair = joined(never, own, moved(own, lambda i: i + 1, even), smap_p, smap_ep)
    pair_other = moved(pair, lambda i: i ^ 2, odd)
    quad = joined(y_even, pair, pair_other, spair_p, spair_op)
    quad_other = moved(quad, lambda i: i ^ 6, odd)
    octet = joined(y_low, quad, quad_other, squad_p, squad_op)
    place3 = ints(x, y < 2, y % 2 == 0)
    behind = lambda v: moved(v, lambda i: i - 8, lambda i: odd(i) and i >= 8)
    got = behind(octet)
    top, sent = hop(place3, 2, zeros, got, soct_p, octet)
    got = behind(sent)
    top, sent = hop(place3, 1, top, got, soct_p, octet)
    got = behind(sent)
    top, sent = descend(place3, 0, top, got, squad_op, quad_other, spair_op, pair_other, smap_p, own)
    got = moved(sent, lambda i: i - 1, odd)
    smoothed = smooth(
        at_core, offsets, upwind, courant, smooth_gain, updates, filtered, top, got
    )
    return filtered, smoothed


def solution(mesh):
    row = P("tm", None)
    in_specs = (P(), row, row, row, row, P("tm", None, None), row, row)
    return jax.shard_map(on_device, mesh=mesh, in_specs=in_specs, out_specs=(row, row), check_vma=False)
```

```python
import jax
import jax.numpy as jnp
from jax import lax
from jax.experimental import pallas as pl
from jax.experimental.pallas import tpu as pltpu
from jax.sharding import PartitionSpec as P


N = 512
OBS = 64
BANDS = 4
REACH = 32
DIFFUSION = 0.25
RELAXATION = 0.02
ROWS = N + 8
LANES = 128
PIECES = N // LANES
CELLS = 32
F32 = jnp.float32
BF16 = jnp.bfloat16
NT = (((1,), (1,)), ((), ()))
NN = (((1,), (0,)), ((), ()))


def lanes(rows, count=N):
    return lax.broadcasted_iota(jnp.int32, (rows, count), 1)


def pieces(v):
    return [v[:, LANES * j : LANES * (j + 1)] for j in range(PIECES)]


def ahead(parts, by):
    turn = jnp.where(by == 0, 0, LANES - by)
    turned = [pltpu.roll(part, turn, 1) for part in parts]
    here = lanes(1, LANES) + by < LANES
    return [jnp.where(here, turned[j], turned[(j + 1) % PIECES]) for j in range(PIECES)]


def neighbours(v):
    lane = lanes(1)
    left = jnp.where(lane > 0, 0.5 * DIFFUSION, 0.0)
    right = jnp.where(lane < N - 1, 0.5 * DIFFUSION, 0.0)
    return right * pltpu.roll(v, N - 1, 1) + left * pltpu.roll(v, 1, 1)


class Step:
    def __init__(self, k, offs_ref, up_ref, c_ref):
        self.offs = [offs_ref[k, band] for band in range(BANDS)]
        self.up = up_ref[pl.ds(k, 1), :]
        courant = c_ref[pl.ds(k, 1), :]
        reach = jnp.full_like(self.up, self.offs[0])
        for band in range(1, BANDS):
            reach = jnp.where(self.up == band, self.offs[band], reach)
        at = lanes(1) + reach
        inside = (at >= 0) & (at < N)
        self.centre = 1.0 - courant - DIFFUSION
        self.advected = jnp.where(inside, courant, 0.0)

    def apply(self, v):
        base = pieces(pltpu.roll(v, REACH, 1))
        ups = pieces(self.up)
        moved = ahead(base, self.offs[0] + REACH)
        for band in range(1, BANDS):
            other = ahead(base, self.offs[band] + REACH)
            moved = [jnp.where(ups[j] == band, other[j], moved[j]) for j in range(PIECES)]
        return self.centre * v + neighbours(v) + self.advected * jnp.concatenate(moved, axis=1)

    def apply_transposed(self, v):
        out = pieces(pltpu.roll(self.advected * v, REACH, 1))
        ups = pieces(pltpu.roll(self.up, REACH, 1))
        total = pieces(self.centre * v + neighbours(v))
        for band in range(BANDS):
            own = [jnp.where(ups[j] == band, out[j], 0.0) for j in range(PIECES)]
            shifted = ahead(own, REACH - self.offs[band])
            total = [total[j] + shifted[j] for j in range(PIECES)]
        return jnp.concatenate(total, axis=1)


def dot(a, b, dims=NN):
    return lax.dot_general(a, b, dims, preferred_element_type=F32)


def split2(v):
    hi = v.astype(BF16)
    return hi, (v - hi.astype(F32)).astype(BF16)


def stacked(v):
    hi = v.astype(BF16).astype(F32)
    return jnp.concatenate([hi, v - hi], axis=0).astype(BF16)


def observed_part(p, s2):
    rows = p.shape[0]
    both = dot(stacked(p), s2, NT)
    return both[:rows] + both[rows:]


def gain_rows(s, gains):
    hi, lo = split2(RELAXATION * s.astype(F32) + gains)
    return jnp.concatenate([hi, hi, lo, lo], axis=0)


def correction(e2, kk):
    hi = e2.astype(BF16).astype(F32)
    mixed = jnp.where(lanes(1, 2 * OBS) >= OBS, e2 - hi, hi)
    return dot(jnp.concatenate([mixed, mixed], axis=1).astype(BF16), kk)


def one_hot(obs_row):
    own = lax.broadcasted_iota(jnp.int32, (OBS, OBS), 0) == lanes(OBS, OBS)
    column = jnp.sum(jnp.where(own, obs_row.astype(F32), 0.0), axis=1, keepdims=True)
    return jnp.where(column.astype(jnp.int32) == lanes(OBS), 1.0, 0.0).astype(BF16)


def through(v, parts_ref):
    rows = v.shape[0]
    both = stacked(v)
    high, low = dot(both, parts_ref[0], NT), dot(both, parts_ref[1], NT)
    return high[:rows] + (high[rows:] + low[:rows] + low[rows:])


def call(kernel, outs, operands, scratch=(), scalars=1, far=0, flops=10**8, moved=1 << 20, limit=16):
    vmem, smem = pl.BlockSpec(memory_space=pltpu.VMEM), pl.BlockSpec(memory_space=pltpu.SMEM)
    anywhere = pl.BlockSpec(memory_space=pltpu.MemorySpace.HBM)
    near_hbm = [
        pltpu.with_memory_space_constraint(value, pltpu.MemorySpace.HBM)
        for value in operands[scalars : scalars + far]
    ]
    return pl.pallas_call(
        kernel,
        out_shape=tuple(jax.ShapeDtypeStruct(*out) for out in outs),
        in_specs=[smem] * scalars + [anywhere] * far + [vmem] * (len(operands) - scalars - far),
        out_specs=(vmem,) * len(outs),
        scratch_shapes=list(scratch),
        cost_estimate=pl.CostEstimate(flops=flops, bytes_accessed=moved, transcendentals=0),
        compiler_params=pltpu.CompilerParams(vmem_limit_bytes=limit << 20),
    )(*operands[:scalars], *near_hbm, *operands[scalars + far :])


PARTS = ((2, N, N), BF16)
VECTOR = ((8, N), F32)


def keep_parts(values_ref, parts_ref):
    for r in range(0, N, 64):
        at = pl.ds(r, 64)
        parts_ref[0, at, :], parts_ref[1, at, :] = split2(values_ref[at, :])


def keep_columns(rows, kept_ref, start):
    turned = jnp.transpose(rows)
    for k in range(rows.shape[0]):
        kept_ref[k, start : start + N, :] = jnp.broadcast_to(turned[:, k : k + 1], (N, LANES))


def clear_edges(padded_ref):
    edge = jnp.zeros((PIECES, REACH, LANES), F32)
    padded_ref[:, 0:REACH, :] = edge
    padded_ref[:, REACH + N : N + 2 * REACH, :] = edge


def start_identity(padded_ref):
    clear_edges(padded_ref)
    row = lax.broadcasted_iota(jnp.int32, (N, LANES), 0)
    for j in range(PIECES):
        padded_ref[j, REACH : REACH + N, :] = jnp.where(row == lanes(N, LANES) + LANES * j, 1.0, 0.0)


def keep_map(padded_ref, map_ref, parts_ref=None):
    for r in range(0, N, 64):
        for j in range(PIECES):
            at, cols = slice(r, r + 64), slice(LANES * j, LANES * (j + 1))
            value = padded_ref[j, REACH + r : REACH + r + 64, :]
            map_ref[at, cols] = value
            if parts_ref is not None:
                parts_ref[0, at, cols], parts_ref[1, at, cols] = split2(value)


def diffused(padded_ref, j, first, size, centre):
    at = lambda by: padded_ref[j, pl.ds(first + by, size), :]
    return centre * at(0) + (0.5 * DIFFUSION) * (at(1) + at(-1))


def filter_map(offsets, upwind, courant, obs_cells, gains, observed):
    steps = offsets.shape[0]

    def kernel(
        offs_ref, cells_ref, up_far, c_far, obs_far, y_far, gains_far,
        map_ref, held_ref, moved_ref, picked_ref, both_ref,
        up_ref, c_ref, obs_ref, y_ref, gains_ref, sem
    ):
        pairs = ((up_far, up_ref), (c_far, c_ref), (obs_far, obs_ref), (y_far, y_ref))
        copies = [pltpu.make_async_copy(a, b, sem.at[i]) for i, (a, b) in enumerate(pairs)]
        for copy in copies:
            copy.start()
        fetch = lambda k: pltpu.make_async_copy(gains_far.at[k], gains_ref.at[k], sem.at[4 + k])
        for k in range(steps):
            fetch(k).start()
        start_identity(held_ref)
        for copy in copies:
            copy.wait()
        keep_columns(up_ref[...].astype(F32) + c_ref[...], both_ref, 0)
        head = lax.broadcasted_iota(jnp.int32, (8, 1), 0) == 0

        def one(k, vec):
            step = Step(k, offs_ref, up_ref, c_ref)
            s = one_hot(obs_ref[pl.ds(k, 1), :])
            fetch(k).wait()
            gain = RELAXATION * s.astype(F32) + gains_ref[k]
            for r in range(0, N, CELLS):
                both = both_ref[k, r : r + CELLS, :]
                ups = jnp.floor(both)
                cs = both - ups
                for j in range(PIECES):
                    at = lambda by: held_ref[j, pl.ds(REACH + r + by, CELLS), :]
                    arrived = at(step.offs[0])
                    for band in range(1, BANDS):
                        arrived = jnp.where(ups == band, at(step.offs[band]), arrived)
                    spread = diffused(held_ref, j, REACH + r, CELLS, 1.0 - cs - DIFFUSION)
                    moved_ref[j, r : r + CELLS, :] = spread + cs * arrived
            for o in range(OBS):
                for j in range(PIECES):
                    cols = slice(LANES * j, LANES * (j + 1))
                    picked_ref[o : o + 1, cols] = moved_ref[j, pl.ds(cells_ref[k, o], 1), :]
            seen_hi, seen_lo = split2(picked_ref[...])
            seen = jnp.concatenate([seen_hi, seen_lo] * 2, axis=0)
            turned = jnp.transpose(jnp.concatenate([gain, gain], axis=0))
            factors = jnp.concatenate(split2(turned), axis=1)
            for r in range(0, N, 256):
                at = slice(r, r + 256)
                corrected = pieces(dot(factors[at], seen))
                for j in range(PIECES):
                    held_ref[j, REACH + r : REACH + r + 256, :] = moved_ref[j, at, :] - corrected[j]

            high, low = split2(gain)
            kk = jnp.concatenate([high, high, low, low], axis=0)
            s2 = jnp.concatenate([s] * 2, axis=0)
            y2 = jnp.concatenate([y_ref[pl.ds(k, 1), :]] * 2, axis=1)
            p = step.apply(vec)
            return p - correction(observed_part(p, s2) - jnp.where(head, y2, 0.0), kk)

        vec = lax.fori_loop(0, steps, one, jnp.zeros((8, N), F32))
        map_ref[N:ROWS, :] = vec
        keep_map(held_ref, map_ref)

    return call(
        kernel,
        (((ROWS, N), F32),),
        (offsets, obs_cells, upwind, courant, obs_cells, observed, gains),
        scratch=[
            pltpu.VMEM((PIECES, N + 2 * REACH, LANES), F32),
            pltpu.VMEM((PIECES, N, LANES), F32),
            pltpu.VMEM((OBS, N), F32),
            pltpu.VMEM((steps, N, LANES), F32),
            pltpu.VMEM((steps, N), jnp.int32),
            pltpu.VMEM((steps, N), F32),
            pltpu.VMEM((steps, OBS), jnp.int32),
            pltpu.VMEM((steps, OBS), F32),
            pltpu.VMEM((steps, OBS, N), F32),
            pltpu.SemaphoreType.DMA((4 + steps,)),
        ],
        scalars=2,
        far=5,
        flops=16 * 10**9,
        moved=4 << 20,
        limit=28,
    )[0]


def smoother_map(offsets, upwind, courant, smooth_gain):
    steps = offsets.shape[0]

    def kernel(offs_ref, up_ref, c_ref, sg_ref, map_ref, parts_ref, held_ref, out_ref, both_ref, gains_ref):
        outside = jnp.full((REACH, LANES), -1.0, F32)
        for k in range(steps):
            both_ref[k, 0:REACH, :] = outside
            both_ref[k, REACH + N : N + 2 * REACH, :] = outside
        keep_columns(up_ref[...].astype(F32) + c_ref[...], both_ref, REACH)
        keep_columns(sg_ref[...], gains_ref, 0)
        start_identity(held_ref.at[0])
        clear_edges(held_ref.at[1])
        clear_edges(out_ref)

        def one(i, carry):
            k = steps - 1 - i
            offs = [offs_ref[k, band] for band in range(BANDS)]
            now, later = held_ref.at[lax.rem(i, 2)], held_ref.at[lax.rem(i + 1, 2)]
            for r in range(0, N, CELLS):
                both = both_ref[k, REACH + r : REACH + r + CELLS, :]
                cs = both - jnp.floor(both)
                for j in range(PIECES):
                    at = slice(REACH + r, REACH + r + CELLS)
                    out_ref[j, at, :] = cs * now[j, at, :]
            for r in range(0, N, CELLS):
                froms = [pl.ds(REACH + r - offs[band], CELLS) for band in range(BANDS)]
                taken = [jnp.floor(both_ref[k, froms[band], :]) == band for band in range(BANDS)]
                both = both_ref[k, REACH + r : REACH + r + CELLS, :]
                centre = 1.0 - (both - jnp.floor(both)) - DIFFUSION
                gain = gains_ref[k, r : r + CELLS, :]
                for j in range(PIECES):
                    total = diffused(now, j, REACH + r, CELLS, centre)
                    for band in range(BANDS):
                        total = total + jnp.where(taken[band], out_ref[j, froms[band], :], 0.0)
                    later[j, REACH + r : REACH + r + CELLS, :] = gain * total
            return carry

        lax.fori_loop(0, steps, one, 0)
        keep_map(held_ref.at[steps % 2], map_ref, parts_ref)

    return call(
        kernel,
        (((N, N), F32), PARTS),
        (offsets, upwind, courant, smooth_gain),
        scratch=[
            pltpu.VMEM((2, PIECES, N + 2 * REACH, LANES), F32),
            pltpu.VMEM((PIECES, N + 2 * REACH, LANES), F32),
            pltpu.VMEM((steps, N + 2 * REACH, LANES), F32),
            pltpu.VMEM((steps, N, LANES), F32),
        ],
        flops=8 * 10**9,
        moved=2 << 20,
        limit=28,
    )


def compose(flag, mine, other, keep=True, parts=False, other_parts=False, far=False):
    rows = mine.shape[0]
    affine = rows > N
    kinds = (("out", keep, ((rows, N), F32)), ("off", affine, VECTOR), ("parts", parts, PARTS), ("other", other_parts, PARTS))

    def kernel(flag_ref, mine_ref, other_ref, *more):
        names = [name for name, wanted, _ in kinds if wanted]
        refs = dict(zip(names, more[: len(names)], strict=True))
        if far:
            *held, sem = more[len(names) :]

            @pl.when(flag_ref[0] != 2)
            def _():
                pairs = enumerate(zip((mine_ref, other_ref), held, strict=True))
                copies = [pltpu.make_async_copy(a, b, sem.at[i]) for i, (a, b) in pairs]
                for copy in copies:
                    copy.start()
                for copy in copies:
                    copy.wait()

            mine_ref, other_ref = held

        def product(first_ref, second_ref):
            if other_parts:
                keep_parts(other_ref, refs["other"])
            high, low = split2(first_ref[0:N, :])
            for start in (0, 256):
                at = pl.ds(start, 256)
                both = stacked(second_ref[at, :])
                big = dot(both, high)
                total = big[:256] + (big[256:] + dot(both[:256], low))
                if keep:
                    refs["out"][at, :] = total
                if parts:
                    refs["parts"][0, at, :], refs["parts"][1, at, :] = split2(total)
            if affine:
                both = stacked(first_ref[N:ROWS, :])
                halves = split2(second_ref[0:N, :])
                big, small = dot(both, halves[0], NT), dot(both, halves[1], NT)
                offset = big[:8] + (big[8:] + small[:8] + small[8:]) + second_ref[N:ROWS, :]
                refs["off"][...] = offset
                if keep:
                    refs["out"][N:ROWS, :] = offset

        @pl.when(flag_ref[0] == 1)
        def _():
            product(other_ref, mine_ref)

        @pl.when(flag_ref[0] == 0)
        def _():
            product(mine_ref, other_ref)

    outs = tuple(shape for _, wanted, shape in kinds if wanted)
    scratch = [pltpu.VMEM((rows, N), F32)] * 2 + [pltpu.SemaphoreType.DMA((2,))]
    return call(
        kernel,
        outs,
        (flag, mine, other),
        scratch=scratch if far else (),
        far=2 if far else 0,
        flops=10**9,
        moved=5 << 20,
    )


def parted(maps):
    def kernel(map_ref, parts_ref, off_ref):
        keep_parts(map_ref, parts_ref)
        off_ref[...] = map_ref[N:ROWS, :]

    return call(kernel, (PARTS, VECTOR), (maps,), scalars=0, flops=10**8, moved=2 << 20)


def hop(place, mark, state, got, parts, offset):
    def kernel(place_ref, state_ref, got_ref, parts_ref, off_ref, new_ref, sent_ref):
        new = jnp.where(place_ref[0] == mark, got_ref[...], state_ref[...])
        new_ref[...] = new
        sent_ref[...] = through(new, parts_ref) + off_ref[...]

    return call(kernel, (VECTOR, VECTOR), (place, state, got, parts, offset))


def descend(place, mark, state, got, quad, quad_off, pair, pair_off, own, own_off):
    def kernel(place_ref, state_ref, got_ref, quad_ref, qo_ref, pair_ref, po_ref, own_ref, oo_ref, new_ref, sent_ref):
        new_ref[...] = jnp.where(place_ref[0] == mark, got_ref[...], state_ref[...])

        @pl.when(place_ref[1] == 1)
        def _():
            new_ref[...] = through(new_ref[...], quad_ref) + qo_ref[...]

        @pl.when(place_ref[2] == 1)
        def _():
            new_ref[...] = through(new_ref[...], pair_ref) + po_ref[...]

        sent_ref[...] = through(new_ref[...], own_ref) + oo_ref[...]

    operands = (place, state, got, quad, quad_off, pair, pair_off, own, own_off)
    return call(kernel, (VECTOR, VECTOR), operands)


def joined(flag, mine, other, my_parts, other_parts):
    def kernel(flag_ref, mine_ref, other_ref, mp_ref, op_ref, out_ref):
        @pl.when(flag_ref[0] == 1)
        def _():
            out_ref[...] = through(other_ref[...], mp_ref) + mine_ref[...]

        @pl.when(flag_ref[0] == 0)
        def _():
            out_ref[...] = through(mine_ref[...], op_ref) + other_ref[...]

    return call(kernel, (VECTOR,), (flag, mine, other, my_parts, other_parts))[0]


def smoothing(steps, diff, offs_ref, up_ref, c_ref, sg_ref, u_ref, store=None):
    def one(i, diff):
        k = steps - 1 - i
        step = Step(k, offs_ref, up_ref, c_ref)
        if store is not None:
            store(k, diff)
        at = pl.ds(k, 1)
        return sg_ref[at, :] * step.apply_transposed(diff + u_ref[at, :])

    return lax.fori_loop(0, steps, one, diff)


def one_hots(obs_cells):
    steps = obs_cells.shape[0]

    def kernel(obs_ref, hots_ref):
        for k in range(steps):
            hots_ref[k] = one_hot(obs_ref[k : k + 1, :])

    return call(kernel, (((steps, OBS, N), BF16),), (obs_cells,), scalars=0)[0]


def forward(place, offsets, upwind, courant, smooth_gain, hots, gains, observed, state, got):
    steps = offsets.shape[0]

    def kernel(
        place_ref, offs_ref, s_far, gains_far, up_ref, c_ref, sg_ref, y_ref, state_ref, got_ref,
        filt_ref, upd_ref, end_ref, s_ref, gains_ref, sem
    ):
        def fetch(k):
            return (
                pltpu.make_async_copy(s_far.at[k], s_ref.at[k], sem.at[k]),
                pltpu.make_async_copy(gains_far.at[k], gains_ref.at[k], sem.at[steps + k]),
            )

        for k in range(steps):
            for copy in fetch(k):
                copy.start()
        first = lax.broadcasted_iota(jnp.int32, (8, 1), 0) == 0

        def one(k, vec):
            step = Step(k, offs_ref, up_ref, c_ref)
            for copy in fetch(k):
                copy.wait()
            s = s_ref[k]
            kk = gain_rows(s, gains_ref[k])
            s2 = jnp.concatenate([s] * 2, axis=0)
            y2 = jnp.concatenate([y_ref[pl.ds(k, 1), :]] * 2, axis=1)
            p = step.apply(vec)
            update = -correction(observed_part(p, s2) - jnp.where(first, y2, 0.0), kk)
            vec = p + update
            filt_ref[pl.ds(k, 1), :] = vec[0:1]
            upd_ref[pl.ds(k, 1), :] = update[0:1]
            return vec

        start = jnp.where(place_ref[0] == 1, got_ref[...], state_ref[...])
        lax.fori_loop(0, steps, one, start)
        zeros = jnp.zeros((8, N), F32)
        end_ref[...] = smoothing(steps, zeros, offs_ref, up_ref, c_ref, sg_ref, upd_ref)

    return call(
        kernel,
        (((steps, N), F32), ((steps, N), F32), VECTOR),
        (place, offsets, hots, gains, upwind, courant, smooth_gain, observed, state, got),
        scratch=[
            pltpu.VMEM((steps, OBS, N), BF16),
            pltpu.VMEM((steps, OBS, N), F32),
            pltpu.SemaphoreType.DMA((2 * steps,)),
        ],
        scalars=2,
        far=2,
        flops=4 * 10**9,
        moved=3 << 20,
    )


def smooth(place, offsets, upwind, courant, smooth_gain, updates, filtered, top, got):
    steps = offsets.shape[0]

    def kernel(place_ref, offs_ref, up_ref, c_ref, sg_ref, u_ref, x_ref, top_ref, got_ref, out_ref):
        def store(k, diff):
            at = pl.ds(k, 1)
            out_ref[at, :] = x_ref[at, :] + diff[0:1]

        diff = jnp.where(place_ref[0] == 0, got_ref[...], top_ref[...])
        smoothing(steps, diff, offs_ref, up_ref, c_ref, sg_ref, u_ref, store)

    return call(
        kernel,
        (((steps, N), F32),),
        (place, offsets, upwind, courant, smooth_gain, updates, filtered, top, got),
        scalars=2,
    )[0]


def on_device(initial, offsets, upwind, courant, obs_cells, gains, observed, smooth_gain):
    place = lax.axis_index("tm")
    x, y, core = place // 8, (place // 2) % 4, place % 2

    def moved(values, to, senders):
        return lax.ppermute(values, "tm", [(i, to(i)) for i in range(32) if senders(i)])

    even = lambda i: i % 2 == 0
    odd = lambda i: i % 2 == 1
    ints = lambda *values: jnp.stack([jnp.asarray(v, jnp.int32) for v in values])
    never = jnp.zeros((1,), jnp.int32)
    at_core = ints(core)
    on_even = lambda flag: ints(jnp.where(core == 0, flag, 2))
    on_odd = lambda flag: ints(jnp.where(core == 1, flag, 2))
    y_even, y_low = ints(y % 2 == 0), ints(y < 2)
    start_row = jnp.broadcast_to(initial[None, :], (8, N))
    zeros = jnp.zeros((8, N), F32)

    after = lambda value, *before: lax.optimization_barrier((value, *before))[0]

    fmap = filter_map(offsets, upwind, courant, obs_cells, gains, observed)
    fmap_odd = moved(fmap, lambda i: i - 1, odd)
    fpair, fpair_o = compose(on_even(0), fmap, fmap_odd)
    fpair_other = moved(fpair, lambda i: i ^ 2, even)
    smap, smap_p = smoother_map(offsets, after(upwind, fpair_o), courant, smooth_gain)
    fquad, fquad_o = compose(on_even(y % 2), fpair, fpair_other)
    fquad_other = moved(fquad, lambda i: i ^ 6, even)
    smap_even = moved(after(smap, fquad_o), lambda i: i + 1, even)
    spair, spair_p, smap_ep = compose(
        on_odd(0), smap, smap_even, parts=True, other_parts=True, far=True
    )
    fpair_op, fpair_oo = parted(fpair_other)
    fmap_p, fmap_o = parted(fmap)
    hots = one_hots(after(obs_cells, fquad_o))
    foct_o, foct_p = compose(after(on_even(y // 2), hots), fquad, fquad_other, keep=False, parts=True)

    place3 = ints(x, y >= 2, y % 2 == 1)
    ahead_of = lambda v: moved(v, lambda i: i + 8, lambda i: even(i) and i < 24)
    state, sent = hop(place3, 0, start_row, start_row, foct_p, foct_o)
    got = ahead_of(sent)
    spair_other = moved(after(spair, sent), lambda i: i ^ 2, odd)
    fquad_op, fquad_oo = parted(fquad_other)
    state, sent = hop(place3, 1, after(state, fquad_oo), got, foct_p, foct_o)
    got = ahead_of(sent)
    state, sent = hop(place3, 2, after(state, fpair_oo, fmap_o), got, foct_p, foct_o)
    got = ahead_of(sent)
    squad, squad_p, spair_op = compose(
        on_odd(1 - y % 2), spair, after(spair_other, sent), parts=True, other_parts=True, far=True
    )
    squad_other = moved(squad, lambda i: i ^ 6, odd)
    state, sent = descend(
        place3, 3, after(state, squad_p), got, fquad_op, fquad_oo, fpair_op, fpair_oo, fmap_p, fmap_o
    )
    got = moved(sent, lambda i: i + 1, even)
    filtered, updates, own = forward(
        at_core, offsets, upwind, courant, smooth_gain, hots, gains, observed, state, got
    )
    soct_p, squad_op = compose(
        on_odd(1 - y // 2),
        squad,
        after(squad_other, own),
        keep=False,
        parts=True,
        other_parts=True,
        far=True,
    )

    pair = joined(never, own, moved(own, lambda i: i + 1, even), smap_p, smap_ep)
    pair_other = moved(pair, lambda i: i ^ 2, odd)
    quad = joined(y_even, pair, pair_other, spair_p, spair_op)
    quad_other = moved(quad, lambda i: i ^ 6, odd)
    octet = joined(y_low, quad, quad_other, squad_p, squad_op)
    place3 = ints(x, y < 2, y % 2 == 0)
    behind = lambda v: moved(v, lambda i: i - 8, lambda i: odd(i) and i >= 8)
    got = behind(octet)
    top, sent = hop(place3, 2, zeros, got, soct_p, octet)
    got = behind(sent)
    top, sent = hop(place3, 1, top, got, soct_p, octet)
    got = behind(sent)
    top, sent = descend(place3, 0, top, got, squad_op, quad_other, spair_op, pair_other, smap_p, own)
    got = moved(sent, lambda i: i - 1, odd)
    smoothed = smooth(
        at_core, offsets, upwind, courant, smooth_gain, updates, filtered, top, got
    )
    return filtered, smoothed


def solution(mesh):
    row = P("tm", None)
    in_specs = (P(), row, row, row, row, P("tm", None, None), row, row)
    return jax.shard_map(on_device, mesh=mesh, in_specs=in_specs, out_specs=(row, row), check_vma=False)
```
